32 devices in a mesh: rows: 16 (over z, y, x), samp: 2 (over core).
Axes of the slice: x: 2, y: 2, z: 4, core: 2. Of those that a mesh axis runs over, the one named last changes fastest.
Arguments:
- samples: float32 [12288, 1024], P('rows', 'samp'), may hold values from -6 to 6
- probes: float32 [12288, 1024], P('rows', 'samp'), may hold values from -6 to 6
- near_blocks: float32 [48, 3, 256, 256], P('rows'), may hold values from -0.375 to 0.375
- near_cols: int32 [48, 3], P('rows'), may hold values from 0 to 47, as said below
- near_count: int32 [48], P('rows'), may hold values from 1 to 3, as said below
- sketch: float32 [1024, 256], P('samp'), may hold values from -0.1875 to 0.1875
Outputs:
- leaf_basis: float32 [12288, 256], P('rows')
- reduced: float32 [4, 16, 256, 1024], P(None, 'rows', None, 'samp')
The draws below stay inside these ranges and needn't reach their ends.
Inputs may be any that keep to these rules, and one draw needn't show every extreme that they name: `near_cols`: slot 0 of block row b names b itself; every slot names a column block within 3 blocks of b; the slots of a row are distinct except near the first and last 3 block rows, where two may repeat. `near_count`: every fourth block row, starting with block row 0, has all 3 slots valid.
All inputs are finite; a program needn't handle non-finite values.
Results may differ from the reference program's by a relative error of at most 0.0003.
Values sent between devices are 32-bit elements; how exact they have to be, the bound alone decides.
No kernel may reach another device: no remote copies, remote signals or barrier semaphores. Data moves between devices by JAX's collectives and lax.ppermute only.
A program may use at most 64 MiB of HBM per device.

```python
import jax
import jax.numpy as jnp
from jax import lax

ROWS_DEV = 768
BLOCK = 256
SLOTS = 3
RANK = 256
SAMPLES = 1024
LEVELS = 4
ORDER = 12288
BLOCKS = 48
REACH = 3
N_ROWS = 16


def draw_samples(key, part):
    first_key = jax.random.fold_in(jax.random.fold_in(key, 11), 0)
    values = jax.random.normal(first_key, (ORDER, SAMPLES), jnp.float32)
    return jnp.clip(values, -6.0, 6.0)


def draw_near_cols(key, part):
    width_all = 2 * REACH
    scores = jax.random.randint(jax.random.fold_in(key, 23), (BLOCKS, width_all), 0, 1 << 20) * width_all + jnp.arange(width_all)[None, :]
    order_ids = jnp.argsort(scores, axis=1, stable=True)
    offsets = jnp.where(order_ids < REACH, order_ids - REACH, order_ids - REACH + 1)
    picked = offsets[:, :SLOTS - 1]
    row_ids = jnp.arange(BLOCKS)[:, None]
    columns = row_ids + picked
    columns = jnp.where((columns < 0) | (columns >= BLOCKS), row_ids - picked, columns)
    return jnp.concatenate([row_ids, columns], axis=1).astype(jnp.int32)


def draw_near_count(key, part):
    counts = jax.random.randint(jax.random.fold_in(key, 37), (BLOCKS,), 1, SLOTS + 1)
    return jnp.where(jnp.arange(BLOCKS) % 4 == 0, SLOTS, counts).astype(jnp.int32)


def block_scale(own_key, dims, shards, least, high):
    gain = 1.0
    for dim, parts in shards:
        draws = jax.random.uniform(jax.random.fold_in(jax.random.fold_in(own_key, 6), dim), (parts,), jnp.float32, least / len(shards), high / len(shards))
        gain = gain * jnp.repeat(jnp.exp(draws), dims[dim] // parts).reshape((-1,) + (1,) * (len(dims) - 1 - dim))
    return gain


def scatter_about(key, shape, scale, reach, cuts=(), dtype=jnp.bfloat16):
    values = jax.random.normal(key, shape, jnp.float32) * scale
    if len(cuts) > 0:
        values = block_scale(key, shape, cuts, -0.22, 0.18) * values
    return jnp.clip(values, min=-reach, max=reach).astype(dtype)


def setup_inputs(seed: int = 0) -> dict:
    keys = jax.random.split(jax.random.key(seed), 7)
    samples = draw_samples(jax.random.fold_in(keys[6], 71), 0)
    probes = scatter_about(keys[1], (ORDER, SAMPLES), 1.0, 6.0, ((0, 16), (1, 2)), jnp.float32)
    near_blocks = scatter_about(keys[2], (BLOCKS, SLOTS, BLOCK, BLOCK), BLOCK ** -0.5, 0.375, ((0, 16),), jnp.float32)
    near_cols = draw_near_cols(jax.random.fold_in(keys[6], 71), 0)
    near_count = draw_near_count(jax.random.fold_in(keys[6], 71), 0)
    sketch = scatter_about(keys[5], (SAMPLES, RANK), SAMPLES ** -0.5, 0.1875, ((0, 2),), jnp.float32)
    return dict(samples=samples, probes=probes, near_blocks=near_blocks, near_cols=near_cols, near_count=near_count, sketch=sketch)


PRECISE = lax.Precision.HIGHEST

def orthonormal_rows(sketched):
    gram_matrix = jnp.dot(sketched.T, sketched, precision=PRECISE)
    lower_factor = jnp.linalg.cholesky(gram_matrix)
    return jax.scipy.linalg.solve_triangular(lower_factor, sketched.T, lower=True)

def reference(samples, probes, near_blocks, near_cols, near_count, sketch):
    probe_blocks = probes.reshape(BLOCKS, BLOCK, SAMPLES)

    def one_block(block_item):
        blocks, column_ids, live_count, row_block = block_item
        pieces = probe_blocks[column_ids]
        live_slots = (jnp.arange(SLOTS) < live_count).astype(jnp.float32)
        pieces = pieces * live_slots[:, None, None]
        return row_block - jnp.einsum('jrc,jcs->rs', blocks, pieces, precision=PRECISE)
    far_samples = lax.map(one_block, (near_blocks, near_cols, near_count, samples.reshape(BLOCKS, BLOCK, SAMPLES)))
    leaf_rows = far_samples.reshape(N_ROWS, ROWS_DEV, SAMPLES)

    def leaf_work(rows_here):
        sketched = jnp.dot(rows_here, sketch, precision=PRECISE)
        basis_t = orthonormal_rows(sketched)
        return (basis_t.T, jnp.dot(basis_t, rows_here, precision=PRECISE))
    bases, current = lax.map(leaf_work, leaf_rows)

    def merge_pair(stacked):
        sketched = jnp.dot(stacked, sketch, precision=PRECISE)
        project_t = orthonormal_rows(sketched)
        return jnp.dot(project_t, stacked, precision=PRECISE)
    levels_out = []
    for height in range(LEVELS):
        paired = current.reshape(-1, 2 * RANK, SAMPLES)
        current = lax.map(merge_pair, paired)
        levels_out.append(jnp.repeat(current, 2 ** (height + 1), axis=0))
    return (bases.reshape(ORDER, RANK), jnp.stack(levels_out))
```

```python
import functools

import jax
import jax.numpy as jnp
from jax import lax
from jax.experimental import pallas as pl
from jax.experimental.pallas import tpu as pltpu
from jax.sharding import PartitionSpec as P

LEVELS = 4
LANES = 128
BASE = 32
NN = ((1,), (0,))
NT = ((1,), (1,))
TN = ((0,), (0,))
HIGH = lax.Precision.HIGH


def split(value):
    high = value.astype(jnp.bfloat16)
    return high, (value - high.astype(jnp.float32)).astype(jnp.bfloat16)


def dot3(left, right, dims):
    lh, ll = split(left)
    rh, rl = split(right)

    def product(a, b):
        return lax.dot_general(a, b, (dims, ((), ())), preferred_element_type=jnp.float32)

    return product(lh, rh) + (product(lh, rl) + product(ll, rh))


def pad_rows(block, start, total):
    parts = []
    if start:
        parts.append(jnp.zeros((start, block.shape[1]), block.dtype))
    parts.append(block)
    rest = total - start - block.shape[0]
    if rest:
        parts.append(jnp.zeros((rest, block.shape[1]), block.dtype))
    return jnp.concatenate(parts, axis=0) if len(parts) > 1 else block


def leaf_factor(work, out, start, base):
    tile = start // LANES * LANES
    off = start - tile
    lane = lax.broadcasted_iota(jnp.int32, (base, LANES), 1)
    row = lax.broadcasted_iota(jnp.int32, (base, LANES), 0)
    col = lane % base
    seg = lane // base
    packed = jnp.where(col == row, 1.0, 0.0)
    for k in range(len(work)):
        block = work[k][start : start + base, tile : tile + LANES]
        shift = (base * k - off) % LANES
        if shift:
            block = pltpu.roll(block, shift, 1)
        packed = jnp.where(seg == k, block, packed)
    pivots = jnp.ones((base, LANES), jnp.float32)
    for j in range(base):
        column = jnp.take_along_axis(packed, seg * base + j, axis=1)
        pivot = column[j : j + 1, :]
        pivots = jnp.where(row == j, pivot, pivots)
        if j == base - 1:
            break
        low = j // 8 * 8
        below = row[low:] > j
        mult = jnp.where(below, column[low:] * (1.0 / pivot), 0.0)
        pivot_row = jnp.where(col[:1] == j, 1.0, packed[j : j + 1, :])
        kept = jnp.where(below & (col[low:] == j), 0.0, packed[low:])
        new = kept - mult * pivot_row
        packed = new if low == 0 else jnp.concatenate([packed[:low], new], axis=0)
    unit = jnp.where(col < row, packed, jnp.where(col == row, 1.0, 0.0))
    unit = unit * lax.rsqrt(pivots)
    inside = (lane >= off) & (lane < off + base)
    for k in range(len(work)):
        shift = (off - base * k) % LANES
        block = pltpu.roll(unit, shift, 1) if shift else unit
        out[k][start : start + base, tile : tile + LANES] = jnp.where(inside, block, 0.0)


def node_factor(work, out, start, size, base):
    if size == base:
        leaf_factor(work, out, start, base)
        return
    half = size // 2
    mid = start + half
    end = start + size
    node_factor(work, out, start, half, base)
    t1 = start // LANES * LANES
    t2 = mid // LANES * LANES
    width = max(LANES, half)
    kept = []
    for k in range(len(work)):
        x1 = out[k][start:mid, t1 : t1 + width]
        l21 = dot3(work[k][mid:end, t1 : t1 + width], x1, NT)
        work[k][mid:end, t2 : t2 + width] -= dot3(l21, pad_rows(l21, mid - t2, width), NT)
        kept.append(dot3(l21, x1, NN))
    node_factor(work, out, mid, half, base)
    for k in range(len(work)):
        x2 = out[k][mid:end, t2 : t2 + width]
        m21 = dot3(x2, pad_rows(kept[k], mid - t2, width), NN)
        out[k][mid:end, t1 : t1 + width] = x2 - m21 if t1 == t2 else -m21


def inverse_kernel(count, size, *refs):
    ins, outs, work = refs[:count], refs[count : 2 * count], refs[2 * count :]
    for k in range(count):
        work[k][...] = ins[k][...]
        for t in range(0, size, LANES):
            outs[k][:, t : t + LANES] = jnp.zeros((size, LANES), jnp.float32)
    node_factor(work, outs, 0, size, BASE)


def factor_inverse(grams):
    count, size = len(grams), grams[0].shape[0]
    spec = pl.BlockSpec(memory_space=pltpu.VMEM)
    return pl.pallas_call(
        functools.partial(inverse_kernel, count, size),
        out_shape=[jax.ShapeDtypeStruct((size, size), jnp.float32)] * count,
        in_specs=[spec] * count,
        out_specs=[spec] * count,
        scratch_shapes=[pltpu.VMEM((size, size), jnp.float32)] * count,
        cost_estimate=pl.CostEstimate(flops=30 * 10**9, bytes_accessed=8 * count * size**2, transcendentals=0),
        name="factor_inverse",
    )(*grams)


def near_kernel(groups, block_count, slot_count, index_ref, count_ref, *refs):
    blocks_ref, base_ref = refs[0], refs[1]
    pieces = refs[2 : 2 + groups]
    out_ref, ext, sems = refs[2 + groups :]
    copies = []
    at = 0
    for g in range(groups):
        depth = pieces[g].shape[0]
        copies.append(pltpu.make_async_copy(pieces[g], ext.at[pl.ds(at, depth)], sems.at[g]))
        at += depth
    for copy in copies:
        copy.start()
    for copy in copies:
        copy.wait()
    size = blocks_ref.shape[2]
    for b in range(block_count):
        rows = pl.ds(b * size, size)
        out_ref[rows, :] = base_ref[rows, :]
        for j in range(slot_count):

            @pl.when(j < count_ref[b])
            def _(b=b, j=j, rows=rows):
                start = pl.multiple_of(index_ref[b, j] * size, size)
                piece = ext[pl.ds(start, size), :]
                out_ref[rows, :] -= dot3(blocks_ref[b, j], piece, NN)


def near_apply(blocks, base, pieces, index, count):
    block_count, slot_count, size, _ = blocks.shape
    rows, width = base.shape
    total = sum(piece.shape[0] for piece in pieces)
    vmem = pl.BlockSpec(memory_space=pltpu.VMEM)
    smem = pl.BlockSpec(memory_space=pltpu.SMEM)
    hbm = pl.BlockSpec(memory_space=pl.ANY)
    return pl.pallas_call(
        functools.partial(near_kernel, len(pieces), block_count, slot_count),
        out_shape=jax.ShapeDtypeStruct((rows, width), jnp.float32),
        in_specs=[smem, smem, vmem, vmem] + [hbm] * len(pieces),
        out_specs=vmem,
        scratch_shapes=[
            pltpu.VMEM((total, width), jnp.float32),
            pltpu.SemaphoreType.DMA((len(pieces),)),
        ],
        cost_estimate=pl.CostEstimate(
            flops=6 * block_count * slot_count * size * size * width,
            bytes_accessed=4 * (total * width + 2 * rows * width + blocks.size),
            transcendentals=0,
        ),
        name="near_apply",
    )(index, count, blocks, base, *pieces)


def across(value, axis, bit):
    return lax.ppermute(value, axis, [(i, i ^ 1 << bit) for i in range(lax.axis_size(axis))])


def relayed(value, axis):
    count = lax.axis_size(axis)
    steps = [(i, i + 2 if i % 2 == 0 else i - 2) for i in range(count)]
    return lax.ppermute(value, axis, [(i, t) for i, t in steps if 0 <= t < count])


def halo(own, parts):
    rows = own.shape[0] // parts
    peer = [across(own[i * rows : (i + 1) * rows], "rows", 0) for i in range(parts)]
    far = [relayed(piece, "rows") for piece in peer]
    return far + [own] + peer


def pick(flag, first, second):
    return jnp.where(flag, second, first)


def shards(samples, probes, near_blocks, near_cols, near_count, sketch):
    rows_dev, samp_dev = samples.shape
    block_size = near_blocks.shape[2]
    block_count = rows_dev // block_size
    rank = sketch.shape[1]
    position = lax.axis_index("rows")
    bits = [position >> h & 1 == 1 for h in range(LEVELS)]
    halves = 2 if lax.axis_size("samp") == 2 else 1
    core = lax.axis_index("samp") % 2 == 1

    index = near_cols - (position * block_count - block_count)
    swapped = jnp.where(index < block_count, index + 2 * block_count, jnp.where(index >= 2 * block_count, index - 2 * block_count, index))
    index = jnp.where(bits[0], swapped, index)

    probe_pieces = halo(probes, block_count)

    if halves == 2:
        width = rank // 2
        turned = pick(core, sketch, jnp.concatenate([sketch[:, width:], sketch[:, :width]], axis=1))
        probe_part = jnp.dot(probes, turned, precision=HIGH)
        sample_part = jnp.dot(samples, turned, precision=HIGH)
        got_probe = across(probe_part[:, width:], "samp", 0)
        got_sample = across(sample_part[:, width:], "samp", 0)
        probe_sketch = probe_part[:, :width] + got_probe
        sample_sketch = sample_part[:, :width] + got_sample
    else:
        width = rank
        probe_sketch = lax.psum(jnp.dot(probes, sketch, precision=HIGH), "samp")
        sample_sketch = lax.psum(jnp.dot(samples, sketch, precision=HIGH), "samp")
    mine = near_apply(near_blocks, sample_sketch, halo(probe_sketch, 1), index, near_count)
    if halves == 2:
        other = across(mine, "samp", 0)
        leaf_sketch = jnp.concatenate([pick(core, mine, other), pick(core, other, mine)], axis=1)
    else:
        leaf_sketch = mine

    gram = jnp.einsum("rk,rl->kl", leaf_sketch, leaf_sketch, precision=HIGH)
    part = pick(core, gram[:, :width], gram[:, rank - width :])
    sums = []
    for h in range(LEVELS):
        part = part + across(part, "rows", h)
        sums.append(part)
    sums = jnp.stack(sums)
    if halves == 2:
        other = across(sums, "samp", 0)
        sums = jnp.concatenate([pick(core, sums, other), pick(core, other, sums)], axis=2)
    (leaf_inverse,) = factor_inverse([gram])
    inverses = factor_inverse([sums[h] for h in range(LEVELS)])
    leaf_basis = lax.dot_general(leaf_sketch, leaf_inverse, (NT, ((), ())), precision=HIGH)

    far_samples = near_apply(near_blocks, samples, probe_pieces, index, near_count)
    product = jnp.einsum("rk,rs->ks", leaf_sketch, far_samples, precision=HIGH)

    def keep_send(value, bit):
        half = value.shape[0] // 2
        return pick(bit, value[:half], value[half:]), pick(bit, value[half:], value[:half])

    def joined(value, bit, level):
        other = across(value, "rows", level)
        return jnp.concatenate([pick(bit, value, other), pick(bit, other, value)], axis=-2)

    keep, send = keep_send(product, bits[0])
    first = keep + across(send, "rows", 0)
    keep, send = keep_send(first, bits[1])
    quarter = keep + across(send, "rows", 1)
    quarters = [quarter]
    for h in range(2, LEVELS):
        quarter = quarter + across(quarter, "rows", h)
        quarters.append(quarter)
    outputs = [joined(first, bits[0], 0)]
    early = joined(joined(jnp.stack(quarters[:2]), bits[1], 1), bits[0], 0)
    outputs += [early[0], early[1]]
    outputs += [joined(joined(value, bits[1], 1), bits[0], 0) for value in quarters[2:]]
    reduced = [jnp.dot(inverse, value, precision=HIGH) for inverse, value in zip(inverses, outputs)]
    return (leaf_basis, jnp.stack(reduced)[:, None, :, :])


def solution(mesh):
    return jax.shard_map(
        shards,
        mesh=mesh,
        in_specs=(
            P("rows", "samp"),
            P("rows", "samp"),
            P("rows", None, None, None),
            P("rows", None),
            P("rows"),
            P("samp", None),
        ),
        out_specs=(P("rows", None), P(None, "rows", None, "samp")),
        check_vma=False,
    )
```

```python
import functools

import jax
import jax.numpy as jnp
from jax import lax
from jax.experimental import pallas as pl
from jax.experimental.pallas import tpu as pltpu
from jax.sharding import PartitionSpec as P

LEVELS = 4
LANES = 128
BASE = 64
WIDE = 16
NN = ((1,), (0,))
NT = ((1,), (1,))
TN = ((0,), (0,))
HIGH = lax.Precision.HIGH


def split(value):
    high = value.astype(jnp.bfloat16)
    return high, (value - high.astype(jnp.float32)).astype(jnp.bfloat16)


def dot3(left, right, dims):
    lh, ll = split(left)
    rh, rl = split(right)

    def product(a, b):
        return lax.dot_general(a, b, (dims, ((), ())), preferred_element_type=jnp.float32)

    return product(lh, rh) + (product(lh, rl) + product(ll, rh))


def pad_rows(block, start, total):
    parts = []
    if start:
        parts.append(jnp.zeros((start, block.shape[1]), block.dtype))
    parts.append(block)
    rest = total - start - block.shape[0]
    if rest:
        parts.append(jnp.zeros((rest, block.shape[1]), block.dtype))
    return jnp.concatenate(parts, axis=0) if len(parts) > 1 else block


def leaf_factor(work, out, start, base):
    fit = LANES // base
    tile = start // LANES * LANES
    off = start - tile
    lane = lax.broadcasted_iota(jnp.int32, (base, LANES), 1)
    row = lax.broadcasted_iota(jnp.int32, (base, LANES), 0)
    col = lane % base
    seg = lane // base
    groups = [range(g, min(g + fit, len(work))) for g in range(0, len(work), fit)]
    packs, pivots = [], []
    for group in groups:
        packed = jnp.where(col == row, 1.0, 0.0)
        for k in group:
            block = work[k][start:start + base, tile:tile + LANES]
            shift = (base * (k % fit) - off) % LANES
            if shift:
                block = pltpu.roll(block, shift, 1)
            packed = jnp.where(seg == k % fit, block, packed)
        packs.append(packed)
        pivots.append(jnp.ones((base, LANES), jnp.float32))
    for first in range(0, base, WIDE):
        low = first // 8 * 8
        rows = row[low:]
        cols = col[low:]
        for g in range(len(groups)):
            active = packs[g][low:]
            columns = [jnp.take_along_axis(active, (seg * base + first + t)[low:], axis=1) for t in range(WIDE)]
            for t in range(WIDE):
                j = first + t
                at = j - low
                pivot = columns[t][at:at + 1, :]
                pivots[g] = jnp.where(row == j, pivot, pivots[g])
                if j == base - 1:
                    break
                mult = jnp.where(rows > j, columns[t] * (1.0 / pivot), 0.0)
                for s in range(t + 1, WIDE):
                    columns[s] = columns[s] - mult * columns[s][at:at + 1, :]
                pivot_row = jnp.where(col[:1] == j, 1.0, active[at:at + 1, :])
                kept = jnp.where((rows > j) & (cols == j), 0.0, active)
                active = kept - mult * pivot_row
            packs[g] = active if low == 0 else jnp.concatenate([packs[g][:low], active], axis=0)
    inside = (lane >= off) & (lane < off + base)
    for g, group in enumerate(groups):
        unit = jnp.where(col < row, packs[g], jnp.where(col == row, 1.0, 0.0))
        unit = unit * lax.rsqrt(pivots[g])
        for k in group:
            shift = (off - base * (k % fit)) % LANES
            block = pltpu.roll(unit, shift, 1) if shift else unit
            out[k][start:start + base, tile:tile + LANES] = jnp.where(inside, block, 0.0)


def node_factor(work, out, start, size, base):
    if size == base:
        leaf_factor(work, out, start, base)
        return
    half = size // 2
    mid = start + half
    end = start + size
    node_factor(work, out, start, half, base)
    t1 = start // LANES * LANES
    t2 = mid // LANES * LANES
    width = max(LANES, half)
    kept = []
    for k in range(len(work)):
        x1 = out[k][start:mid, t1 : t1 + width]
        l21 = dot3(work[k][mid:end, t1 : t1 + width], x1, NT)
        work[k][mid:end, t2 : t2 + width] -= dot3(l21, pad_rows(l21, mid - t2, width), NT)
        kept.append(dot3(l21, x1, NN))
    node_factor(work, out, mid, half, base)
    for k in range(len(work)):
        x2 = out[k][mid:end, t2 : t2 + width]
        m21 = dot3(x2, pad_rows(kept[k], mid - t2, width), NN)
        out[k][mid:end, t1 : t1 + width] = x2 - m21 if t1 == t2 else -m21


def inverse_kernel(count, size, *refs):
    ins, outs, work = refs[:count], refs[count : 2 * count], refs[2 * count :]
    for k in range(count):
        work[k][...] = ins[k][...]
        for t in range(0, size, LANES):
            outs[k][:, t : t + LANES] = jnp.zeros((size, LANES), jnp.float32)
    node_factor(work, outs, 0, size, BASE)


def factor_inverse(grams):
    count, size = len(grams), grams[0].shape[0]
    spec = pl.BlockSpec(memory_space=pltpu.VMEM)
    return pl.pallas_call(
        functools.partial(inverse_kernel, count, size),
        out_shape=[jax.ShapeDtypeStruct((size, size), jnp.float32)] * count,
        in_specs=[spec] * count,
        out_specs=[spec] * count,
        scratch_shapes=[pltpu.VMEM((size, size), jnp.float32)] * count,
        cost_estimate=pl.CostEstimate(flops=15 * 10**9, bytes_accessed=8 * count * size**2, transcendentals=0),
        name="factor_inverse",
    )(*grams)


def near_kernel(groups, block_count, slot_count, index_ref, count_ref, *refs):
    blocks_ref, base_ref = refs[0], refs[1]
    pieces = refs[2 : 2 + groups]
    out_ref, ext, sems = refs[2 + groups :]
    copies = []
    at = 0
    for g in range(groups):
        depth = pieces[g].shape[0]
        copies.append(pltpu.make_async_copy(pieces[g], ext.at[pl.ds(at, depth)], sems.at[g]))
        at += depth
    for copy in copies:
        copy.start()
    for copy in copies:
        copy.wait()
    size = blocks_ref.shape[2]
    for b in range(block_count):
        rows = pl.ds(b * size, size)
        out_ref[rows, :] = base_ref[rows, :]
        for j in range(slot_count):

            @pl.when(j < count_ref[b])
            def _(b=b, j=j, rows=rows):
                start = pl.multiple_of(index_ref[b, j] * size, size)
                piece = ext[pl.ds(start, size), :]
                out_ref[rows, :] -= dot3(blocks_ref[b, j], piece, NN)


def near_apply(blocks, base, pieces, index, count):
    block_count, slot_count, size, _ = blocks.shape
    rows, width = base.shape
    total = sum(piece.shape[0] for piece in pieces)
    vmem = pl.BlockSpec(memory_space=pltpu.VMEM)
    smem = pl.BlockSpec(memory_space=pltpu.SMEM)
    hbm = pl.BlockSpec(memory_space=pl.ANY)
    return pl.pallas_call(
        functools.partial(near_kernel, len(pieces), block_count, slot_count),
        out_shape=jax.ShapeDtypeStruct((rows, width), jnp.float32),
        in_specs=[smem, smem, vmem, vmem] + [hbm] * len(pieces),
        out_specs=vmem,
        scratch_shapes=[
            pltpu.VMEM((total, width), jnp.float32),
            pltpu.SemaphoreType.DMA((len(pieces),)),
        ],
        cost_estimate=pl.CostEstimate(
            flops=6 * block_count * slot_count * size * size * width,
            bytes_accessed=4 * (total * width + 2 * rows * width + blocks.size),
            transcendentals=0,
        ),
        name="near_apply",
    )(index, count, blocks, base, *pieces)


def fold_kernel(index_ref, count_ref, blocks_ref, sketch_ref, out_ref):
    block_count, slot_count, size, _ = blocks_ref.shape
    out_ref[...] = jnp.zeros(out_ref.shape, jnp.float32)
    for b in range(block_count):
        for j in range(slot_count):

            @pl.when(j < count_ref[b])
            def _(b=b, j=j):
                target = pl.ds(pl.multiple_of(index_ref[b, j] * size, size), size)
                rows = pl.ds(b * size, size)
                out_ref[target, :] += dot3(blocks_ref[b, j], sketch_ref[rows, :], TN)


def near_fold(blocks, sketch, index, count, total):
    block_count, slot_count, size, _ = blocks.shape
    rank = sketch.shape[1]
    vmem = pl.BlockSpec(memory_space=pltpu.VMEM)
    smem = pl.BlockSpec(memory_space=pltpu.SMEM)
    return pl.pallas_call(
        fold_kernel,
        out_shape=jax.ShapeDtypeStruct((total, rank), jnp.float32),
        in_specs=[smem, smem, vmem, vmem],
        out_specs=vmem,
        cost_estimate=pl.CostEstimate(
            flops=6 * block_count * slot_count * size * size * rank,
            bytes_accessed=4 * (total * rank + sketch.size + blocks.size),
            transcendentals=0,
        ),
        name="near_fold",
    )(index, count, blocks, sketch)


def across(value, axis, bit):
    return lax.ppermute(value, axis, [(i, i ^ 1 << bit) for i in range(lax.axis_size(axis))])


def relayed(value, axis):
    count = lax.axis_size(axis)
    steps = [(i, i + 2 if i % 2 == 0 else i - 2) for i in range(count)]
    return lax.ppermute(value, axis, [(i, t) for i, t in steps if 0 <= t < count])


def halo(own, parts):
    rows = own.shape[0] // parts
    peer = [across(own[i * rows : (i + 1) * rows], "rows", 0) for i in range(parts)]
    far = [relayed(piece, "rows") for piece in peer]
    return far + [own] + peer


def pick(flag, first, second):
    return jnp.where(flag, second, first)


def shards(samples, probes, near_blocks, near_cols, near_count, sketch):
    rows_dev, samp_dev = samples.shape
    block_size = near_blocks.shape[2]
    block_count = rows_dev // block_size
    rank = sketch.shape[1]
    position = lax.axis_index("rows")
    bits = [position >> h & 1 == 1 for h in range(LEVELS)]
    halves = 2 if lax.axis_size("samp") == 2 else 1
    core = lax.axis_index("samp") % 2 == 1

    index = near_cols - (position * block_count - block_count)
    swapped = jnp.where(index < block_count, index + 2 * block_count, jnp.where(index >= 2 * block_count, index - 2 * block_count, index))
    index = jnp.where(bits[0], swapped, index)

    if halves == 2:
        width = rank // 2
        turned = pick(core, sketch, jnp.concatenate([sketch[:, width:], sketch[:, :width]], axis=1))
        probe_part = jnp.dot(probes, turned, precision=HIGH)
        sample_part = jnp.dot(samples, turned, precision=HIGH)
        got_probe = across(probe_part[:, width:], "samp", 0)
        got_sample = across(sample_part[:, width:], "samp", 0)
        probe_sketch = probe_part[:, :width] + got_probe
        sample_sketch = sample_part[:, :width] + got_sample
    else:
        width = rank
        probe_sketch = lax.psum(jnp.dot(probes, sketch, precision=HIGH), "samp")
        sample_sketch = lax.psum(jnp.dot(samples, sketch, precision=HIGH), "samp")
    mine = near_apply(near_blocks, sample_sketch, halo(probe_sketch, 1), index, near_count)
    if halves == 2:
        other = across(mine, "samp", 0)
        leaf_sketch = jnp.concatenate([pick(core, mine, other), pick(core, other, mine)], axis=1)
    else:
        leaf_sketch = mine

    gram = jnp.einsum("rk,rl->kl", leaf_sketch, leaf_sketch, precision=HIGH)
    part = pick(core, gram[:, :width], gram[:, rank - width :])
    sums = []
    for h in range(LEVELS):
        part = part + across(part, "rows", h)
        sums.append(part)
    sums = jnp.stack(sums)
    if halves == 2:
        other = across(sums, "samp", 0)
        sums = jnp.concatenate([pick(core, sums, other), pick(core, other, sums)], axis=2)
    leaf_inverse, *inverses = factor_inverse([gram] + [sums[h] for h in range(LEVELS)])
    leaf_basis = lax.dot_general(leaf_sketch, leaf_inverse, (NT, ((), ())), precision=HIGH)

    folded = near_fold(near_blocks, leaf_sketch, index, near_count, 3 * rows_dev)

    def transposed(left, right):
        return lax.dot_general(left, right, (TN, ((), ())), precision=HIGH)

    pieces = halo(probes, block_count)
    product = transposed(leaf_sketch, samples)
    at = 0
    terms = []
    for piece in pieces:
        depth = piece.shape[0]
        terms.append(transposed(folded[at : at + depth], piece))
        at += depth
    parts = len(terms) // 2
    for i in [parts] + [i for p in range(parts) for i in (parts + 1 + p, p)]:
        product = product - terms[i]

    def keep_send(value, bit):
        half = value.shape[0] // 2
        return pick(bit, value[:half], value[half:]), pick(bit, value[half:], value[:half])

    def joined(value, bit, level):
        other = across(value, "rows", level)
        return jnp.concatenate([pick(bit, value, other), pick(bit, other, value)], axis=-2)

    keep, send = keep_send(product, bits[0])
    first = keep + across(send, "rows", 0)
    keep, send = keep_send(first, bits[1])
    quarter = keep + across(send, "rows", 1)
    quarters = [quarter]
    for h in range(2, LEVELS):
        quarter = quarter + across(quarter, "rows", h)
        quarters.append(quarter)
    outputs = [joined(first, bits[0], 0)]
    early = joined(joined(jnp.stack(quarters[:2]), bits[1], 1), bits[0], 0)
    outputs += [early[0], early[1]]
    outputs += [joined(joined(value, bits[1], 1), bits[0], 0) for value in quarters[2:]]
    reduced = [jnp.dot(inverse, value, precision=HIGH) for inverse, value in zip(inverses, outputs)]
    return (leaf_basis, jnp.stack(reduced)[:, None, :, :])


def solution(mesh):
    return jax.shard_map(
        shards,
        mesh=mesh,
        in_specs=(
            P("rows", "samp"),
            P("rows", "samp"),
            P("rows", None, None, None),
            P("rows", None),
            P("rows"),
            P("samp", None),
        ),
        out_specs=(P("rows", None), P(None, "rows", None, "samp")),
        check_vma=False,
    )
```

```python
import functools

import jax
import jax.numpy as jnp
from jax import lax
from jax.experimental import pallas as pl
from jax.experimental.pallas import tpu as pltpu
from jax.sharding import PartitionSpec as P

LEVELS = 4
LANES = 128
BASE = 64
WIDE = 16
NN = ((1,), (0,))
NT = ((1,), (1,))
HIGH = lax.Precision.HIGH


def split(value):
    high = value.astype(jnp.bfloat16)
    return high, (value - high.astype(jnp.float32)).astype(jnp.bfloat16)


def dot3(left, right, dims):
    lh, ll = split(left)
    rh, rl = split(right)

    def product(a, b):
        return lax.dot_general(a, b, (dims, ((), ())), preferred_element_type=jnp.float32)

    return product(lh, rh) + (product(lh, rl) + product(ll, rh))


def pad_rows(block, start, total):
    parts = []
    if start:
        parts.append(jnp.zeros((start, block.shape[1]), block.dtype))
    parts.append(block)
    rest = total - start - block.shape[0]
    if rest:
        parts.append(jnp.zeros((rest, block.shape[1]), block.dtype))
    return jnp.concatenate(parts, axis=0) if len(parts) > 1 else block


def leaf_factor(work, out, start, base):
    fit = LANES // base
    tile = start // LANES * LANES
    off = start - tile
    lane = lax.broadcasted_iota(jnp.int32, (base, LANES), 1)
    row = lax.broadcasted_iota(jnp.int32, (base, LANES), 0)
    col = lane % base
    seg = lane // base
    groups = [range(g, min(g + fit, len(work))) for g in range(0, len(work), fit)]
    packs, pivots = [], []
    for group in groups:
        packed = jnp.where(col == row, 1.0, 0.0)
        for k in group:
            block = work[k][start:start + base, tile:tile + LANES]
            shift = (base * (k % fit) - off) % LANES
            if shift:
                block = pltpu.roll(block, shift, 1)
            packed = jnp.where(seg == k % fit, block, packed)
        packs.append(packed)
        pivots.append(jnp.ones((base, LANES), jnp.float32))
    for first in range(0, base, WIDE):
        low = first // 8 * 8
        rows = row[low:]
        cols = col[low:]
        for g in range(len(groups)):
            active = packs[g][low:]
            columns = [jnp.take_along_axis(active, (seg * base + first + t)[low:], axis=1) for t in range(WIDE)]
            for t in range(WIDE):
                j = first + t
                at = j - low
                pivot = columns[t][at:at + 1, :]
                pivots[g] = jnp.where(row == j, pivot, pivots[g])
                if j == base - 1:
                    break
                mult = jnp.where(rows > j, columns[t] * (1.0 / pivot), 0.0)
                for s in range(t + 1, WIDE):
                    columns[s] = columns[s] - mult * columns[s][at:at + 1, :]
                pivot_row = jnp.where(col[:1] == j, 1.0, active[at:at + 1, :])
                kept = jnp.where((rows > j) & (cols == j), 0.0, active)
                active = kept - mult * pivot_row
            packs[g] = active if low == 0 else jnp.concatenate([packs[g][:low], active], axis=0)
    inside = (lane >= off) & (lane < off + base)
    for g, group in enumerate(groups):
        unit = jnp.where(col < row, packs[g], jnp.where(col == row, 1.0, 0.0))
        unit = unit * lax.rsqrt(pivots[g])
        for k in group:
            shift = (off - base * (k % fit)) % LANES
            block = pltpu.roll(unit, shift, 1) if shift else unit
            out[k][start:start + base, tile:tile + LANES] = jnp.where(inside, block, 0.0)


def node_factor(work, out, start, size, base):
    if size == base:
        leaf_factor(work, out, start, base)
        return
    half = size // 2
    mid = start + half
    end = start + size
    node_factor(work, out, start, half, base)
    t1 = start // LANES * LANES
    t2 = mid // LANES * LANES
    width = max(LANES, half)
    kept = []
    for k in range(len(work)):
        x1 = out[k][start:mid, t1 : t1 + width]
        l21 = dot3(work[k][mid:end, t1 : t1 + width], x1, NT)
        work[k][mid:end, t2 : t2 + width] -= dot3(l21, pad_rows(l21, mid - t2, width), NT)
        kept.append(dot3(l21, x1, NN))
    node_factor(work, out, mid, half, base)
    for k in range(len(work)):
        x2 = out[k][mid:end, t2 : t2 + width]
        m21 = dot3(x2, pad_rows(kept[k], mid - t2, width), NN)
        out[k][mid:end, t1 : t1 + width] = x2 - m21 if t1 == t2 else -m21


def first_kernel(size, core_ref, gram_ref, mine_ref, other_ref, *refs):
    count = mine_ref.shape[0] + 1
    inverse, rest, kept = refs[:count], refs[count : 2 * count], refs[2 * count : 3 * count]
    work = refs[3 * count :]
    width = mine_ref.shape[2]
    half = size // 2
    swap = core_ref[0] == 1
    for k in range(count):
        if k == 0:
            work[k][...] = gram_ref[...]
        elif width == size:
            work[k][...] = mine_ref[k - 1]
        else:
            mine, other = mine_ref[k - 1], other_ref[k - 1]
            work[k][:, :width] = jnp.where(swap, other, mine)
            work[k][:, width:] = jnp.where(swap, mine, other)
        for t in range(0, half, LANES):
            inverse[k][:, t : t + LANES] = jnp.zeros((half, LANES), jnp.float32)
    node_factor(work, inverse, 0, half, BASE)
    for k in range(count):
        x1 = inverse[k][...]
        l21 = dot3(work[k][half:, :half], x1, NT)
        rest[k][...] = work[k][half:, half:] - dot3(l21, l21, NT)
        kept[k][...] = dot3(l21, x1, NN)


def second_kernel(count, half, *refs):
    inverse, rest, kept = refs[:count], refs[count : 2 * count], refs[2 * count : 3 * count]
    out = refs[3 * count : 4 * count]
    work, second = refs[4 * count : 5 * count], refs[5 * count :]
    for k in range(count):
        work[k][...] = rest[k][...]
        for t in range(0, half, LANES):
            second[k][:, t : t + LANES] = jnp.zeros((half, LANES), jnp.float32)
        out[k][:half, :half] = inverse[k][...]
        out[k][:half, half:] = jnp.zeros((half, half), jnp.float32)
    node_factor(work, second, 0, half, BASE)
    for k in range(count):
        x2 = second[k][...]
        out[k][half:, half:] = x2
        out[k][half:, :half] = -dot3(x2, kept[k][...], NN)


def factor_first(core, gram, mine, other):
    count, size = mine.shape[0] + 1, gram.shape[0]
    half = size // 2
    vmem = pl.BlockSpec(memory_space=pltpu.VMEM)
    smem = pl.BlockSpec(memory_space=pltpu.SMEM)
    return pl.pallas_call(
        functools.partial(first_kernel, size),
        out_shape=[jax.ShapeDtypeStruct((half, half), jnp.float32)] * (3 * count),
        in_specs=[smem, vmem, vmem, vmem],
        out_specs=[vmem] * (3 * count),
        scratch_shapes=[pltpu.VMEM((size, size), jnp.float32)] * count,
        cost_estimate=pl.CostEstimate(flops=7 * 10**9, bytes_accessed=8 * count * size**2, transcendentals=0),
        name="factor_first",
    )(core, gram, mine, other)


def factor_second(parts):
    count, half = len(parts) // 3, parts[0].shape[0]
    vmem = pl.BlockSpec(memory_space=pltpu.VMEM)
    return pl.pallas_call(
        functools.partial(second_kernel, count, half),
        out_shape=[jax.ShapeDtypeStruct((2 * half, 2 * half), jnp.float32)] * count,
        in_specs=[vmem] * (3 * count),
        out_specs=[vmem] * count,
        scratch_shapes=[pltpu.VMEM((half, half), jnp.float32)] * (2 * count),
        cost_estimate=pl.CostEstimate(flops=7 * 10**9, bytes_accessed=32 * count * half**2, transcendentals=0),
        name="factor_second",
    )(*parts)


def near_kernel(groups, block_count, slot_count, index_ref, count_ref, *refs):
    blocks_ref, base_ref = refs[0], refs[1]
    pieces = refs[2 : 2 + groups]
    out_ref, ext, sems = refs[2 + groups :]
    copies = []
    at = 0
    for g in range(groups):
        depth = pieces[g].shape[0]
        copies.append(pltpu.make_async_copy(pieces[g], ext.at[pl.ds(at, depth)], sems.at[g]))
        at += depth
    for copy in copies:
        copy.start()
    for copy in copies:
        copy.wait()
    size = blocks_ref.shape[2]
    for b in range(block_count):
        rows = pl.ds(b * size, size)
        total = base_ref[rows, :]
        for j in range(slot_count):
            start = pl.multiple_of(index_ref[b, j] * size, size)
            piece = jnp.where(j < count_ref[b], ext[pl.ds(start, size), :], 0.0)
            total = total - dot3(blocks_ref[b, j], piece, NN)
        out_ref[rows, :] = total


def near_apply(blocks, base, pieces, index, count):
    block_count, slot_count, size, _ = blocks.shape
    rows, width = base.shape
    total = sum(piece.shape[0] for piece in pieces)
    vmem = pl.BlockSpec(memory_space=pltpu.VMEM)
    smem = pl.BlockSpec(memory_space=pltpu.SMEM)
    hbm = pl.BlockSpec(memory_space=pl.ANY)
    return pl.pallas_call(
        functools.partial(near_kernel, len(pieces), block_count, slot_count),
        out_shape=jax.ShapeDtypeStruct((rows, width), jnp.float32),
        in_specs=[smem, smem, vmem, vmem] + [hbm] * len(pieces),
        out_specs=vmem,
        scratch_shapes=[
            pltpu.VMEM((total, width), jnp.float32),
            pltpu.SemaphoreType.DMA((len(pieces),)),
        ],
        cost_estimate=pl.CostEstimate(
            flops=6 * block_count * slot_count * size * size * width,
            bytes_accessed=4 * (total * width + 2 * rows * width + blocks.size),
            transcendentals=0,
        ),
        name="near_apply",
    )(index, count, blocks, base, *pieces)


def leaf_kernel(core_ref, mine_ref, other_ref, sketch_ref, turned_ref, gram_ref, part_ref):
    width = mine_ref.shape[1]
    if width == gram_ref.shape[0]:
        sketch = mine_ref[...]
    else:
        swap = core_ref[0] == 1
        mine, other = mine_ref[...], other_ref[...]
        sketch = jnp.concatenate([jnp.where(swap, other, mine), jnp.where(swap, mine, other)], axis=1)
    sketch_ref[...] = sketch
    turned = sketch.T
    turned_ref[...] = turned
    gram = dot3(turned, sketch, NN)
    gram_ref[...] = gram
    rank = gram.shape[0]
    part_ref[...] = jnp.where(core_ref[0] == 1, gram[:, rank - width :], gram[:, :width])


def leaf_products(core, mine, other, rank):
    rows, width = mine.shape
    vmem = pl.BlockSpec(memory_space=pltpu.VMEM)
    smem = pl.BlockSpec(memory_space=pltpu.SMEM)
    shapes = [(rows, rank), (rank, rows), (rank, rank), (rank, width)]
    return pl.pallas_call(
        leaf_kernel,
        out_shape=[jax.ShapeDtypeStruct(shape, jnp.float32) for shape in shapes],
        in_specs=[smem, vmem, vmem],
        out_specs=[vmem] * 4,
        cost_estimate=pl.CostEstimate(flops=6 * rows * rank * rank, bytes_accessed=16 * rows * rank, transcendentals=0),
        name="leaf_products",
    )(core, mine, other)


def fold_kernel(index_ref, count_ref, blocks_ref, turned_ref, out_ref):
    block_count, slot_count, size, _ = blocks_ref.shape
    out_ref[...] = jnp.zeros(out_ref.shape, jnp.float32)
    for b in range(block_count):
        turned = turned_ref[:, b * size : (b + 1) * size]
        for j in range(slot_count):
            block = jnp.where(j < count_ref[b], blocks_ref[b, j], 0.0)
            out_ref[index_ref[b, j]] -= dot3(turned, block, NN)


def near_fold(blocks, turned, index, count):
    block_count, slot_count, size, _ = blocks.shape
    rank = turned.shape[0]
    vmem = pl.BlockSpec(memory_space=pltpu.VMEM)
    smem = pl.BlockSpec(memory_space=pltpu.SMEM)
    return pl.pallas_call(
        fold_kernel,
        out_shape=jax.ShapeDtypeStruct((3 * block_count, rank, size), jnp.float32),
        in_specs=[smem, smem, vmem, vmem],
        out_specs=vmem,
        cost_estimate=pl.CostEstimate(
            flops=6 * block_count * slot_count * size * size * rank,
            bytes_accessed=4 * (turned.size + blocks.size + 3 * block_count * rank * size),
            transcendentals=0,
        ),
        name="near_fold",
    )(index, count, blocks, turned)


def reduce_kernel(place_ref, *refs):
    count = LEVELS
    inverses, first, first_other = refs[:count], refs[count], refs[count + 1]
    early, last = refs[count + 2 : count + 6], refs[count + 6 : count + 10]
    out_ref, stage = refs[count + 10 :]
    rank = inverses[0].shape[0]
    half, quarter = rank // 2, rank // 4
    for h in range(count):
        if h == 0:
            parts = [(half, first[...], 0), (half, first_other[...], 1)]
        elif h < count - 1:
            parts = [(quarter, early[i][h - 1], 2 + i) for i in range(4)]
        else:
            parts = [(quarter, last[i][...], 2 + i) for i in range(4)]
        for depth, value, at in parts:
            stage[h, pl.ds(pl.multiple_of(place_ref[at], depth), depth), :] = value
    for h in range(count):
        out_ref[h, 0] = dot3(inverses[h][...], stage[h], NN)


def reduce_all(place, inverses, first, early, last):
    rank, width = inverses[0].shape[0], last[0].shape[1]
    vmem = pl.BlockSpec(memory_space=pltpu.VMEM)
    smem = pl.BlockSpec(memory_space=pltpu.SMEM)
    args = [*inverses, *first, *early, *last]
    return pl.pallas_call(
        reduce_kernel,
        out_shape=jax.ShapeDtypeStruct((LEVELS, 1, rank, width), jnp.float32),
        in_specs=[smem] + [vmem] * len(args),
        out_specs=vmem,
        scratch_shapes=[pltpu.VMEM((LEVELS, rank, width), jnp.float32)],
        cost_estimate=pl.CostEstimate(
            flops=6 * LEVELS * rank * rank * width, bytes_accessed=8 * LEVELS * rank * (rank + width), transcendentals=0
        ),
        name="reduce_all",
    )(place, *args)


def across(value, axis, bit):
    return lax.ppermute(value, axis, [(i, i ^ 1 << bit) for i in range(lax.axis_size(axis))])


def relayed(value, axis):
    count = lax.axis_size(axis)
    steps = [(i, i + 2 if i % 2 == 0 else i - 2) for i in range(count)]
    return lax.ppermute(value, axis, [(i, t) for i, t in steps if 0 <= t < count])


def pick(flag, first, second):
    return jnp.where(flag, second, first)


def halves_of(value, bit):
    half = value.shape[0] // 2
    return pick(bit, value[:half], value[half:]), pick(bit, value[half:], value[:half])


def leaf_and_levels(samples, probes, near_blocks, near_cols, near_count, sketch):
    rows_dev, _ = samples.shape
    block_size = near_blocks.shape[2]
    block_count = rows_dev // block_size
    rank = sketch.shape[1]
    position = lax.axis_index("rows")
    bits = [position >> h & 1 for h in range(LEVELS)]
    odd = bits[0] == 1
    upper = bits[1] == 1
    halves = 2 if lax.axis_size("samp") == 2 else 1
    core = lax.axis_index("samp") % 2
    core_flag = core.reshape(1).astype(jnp.int32)

    index = near_cols - (position * block_count - block_count)
    moved = jnp.where(index < block_count, 2 * block_count, jnp.where(index >= 2 * block_count, -2 * block_count, 0))
    index = index + jnp.where(odd, moved, 0)

    blocks = [probes[i * block_size : (i + 1) * block_size] for i in range(block_count)]
    peer = [across(blocks[i], "rows", 0) for i in range(block_count)]
    far = [relayed(peer[i], "rows") for i in range(block_count)]

    if halves == 2:
        width = rank // 2
        turned_sketch = pick(core == 1, sketch, jnp.concatenate([sketch[:, width:], sketch[:, :width]], axis=1))
        probe_part = jnp.dot(probes, turned_sketch, precision=HIGH)
        sample_part = jnp.dot(samples, turned_sketch, precision=HIGH)
        probe_sketch = probe_part[:, :width] + across(probe_part[:, width:], "samp", 0)
        sample_sketch = sample_part[:, :width] + across(sample_part[:, width:], "samp", 0)
    else:
        probe_sketch = lax.psum(jnp.dot(probes, sketch, precision=HIGH), "samp")
        sample_sketch = lax.psum(jnp.dot(samples, sketch, precision=HIGH), "samp")
    peer_sketch = across(probe_sketch, "rows", 0)
    far_sketch = relayed(peer_sketch, "rows")
    mine = near_apply(near_blocks, sample_sketch, [far_sketch, probe_sketch, peer_sketch], index, near_count)
    other = across(mine, "samp", 0) if halves == 2 else mine
    leaf_sketch, turned, gram, part = leaf_products(core_flag, mine, other, rank)

    sums = []
    for h in range(LEVELS):
        part = part + across(part, "rows", h)
        sums.append(part)
    sums = jnp.stack(sums)
    sums_other = across(sums, "samp", 0) if halves == 2 else sums
    parts = factor_first(core_flag, gram, sums, sums_other)
    leaf_inverse, *inverses = factor_second(parts)
    leaf_basis = lax.dot_general(leaf_sketch, leaf_inverse, (NT, ((), ())), precision=HIGH)

    folded = near_fold(near_blocks, turned, index, near_count)

    def times(left, right):
        return jnp.dot(left, right, precision=HIGH)

    product = times(turned, samples)
    for i in range(block_count):
        product = product + times(folded[block_count + i], blocks[i])
    for i in range(block_count):
        product = product + times(folded[2 * block_count + i], peer[i])
    for i in range(block_count):
        product = product + times(folded[i], far[i])

    keep, send = halves_of(product, odd)
    first = keep + across(send, "rows", 0)
    first_other = across(first, "rows", 0)
    keep, send = halves_of(first, upper)
    quarter = keep + across(send, "rows", 1)
    quarters = [quarter]
    for h in range(2, LEVELS):
        quarter = quarter + across(quarter, "rows", h)
        quarters.append(quarter)

    def gathered(value):
        along = across(value, "rows", 1)
        beside = across(value, "rows", 0)
        diagonal = across(along, "rows", 0)
        return [value, along, beside, diagonal]

    early = gathered(jnp.stack(quarters[:-1]))
    last = gathered(quarters[-1])
    half = rank // 2
    x, y = bits[0] * half, bits[1] * (half // 2)
    fx, fy = half - x, half // 2 - y
    place = jnp.stack([x, fx, x + y, x + fy, fx + y, fx + fy]).astype(jnp.int32)
    reduced = reduce_all(place, inverses, [first, first_other], early, last)
    return (leaf_basis, reduced)


def solution(mesh):
    return jax.shard_map(
        leaf_and_levels,
        mesh=mesh,
        in_specs=(
            P("rows", "samp"),
            P("rows", "samp"),
            P("rows", None, None, None),
            P("rows", None),
            P("rows"),
            P("samp", None),
        ),
        out_specs=(P("rows", None), P(None, "rows", None, "samp")),
        check_vma=False,
    )
```

```python
import functools

import jax
import jax.numpy as jnp
from jax import lax
from jax.experimental import pallas as pl
from jax.experimental.pallas import tpu as pltpu
from jax.sharding import PartitionSpec as P

LEVELS = 4
LANES = 128
BASE = 64
WIDE = 16
SPLIT = 2
NN = ((1,), (0,))
NT = ((1,), (1,))
HIGH = lax.Precision.HIGH


def split(value):
    high = value.astype(jnp.bfloat16)
    return high, (value - high.astype(jnp.float32)).astype(jnp.bfloat16)


def dot3(left, right, dims):
    lh, ll = split(left)
    rh, rl = split(right)

    def product(a, b):
        return lax.dot_general(a, b, (dims, ((), ())), preferred_element_type=jnp.float32)

    return product(lh, rh) + (product(lh, rl) + product(ll, rh))


def pad_rows(block, start, total):
    parts = []
    if start:
        parts.append(jnp.zeros((start, block.shape[1]), block.dtype))
    parts.append(block)
    rest = total - start - block.shape[0]
    if rest:
        parts.append(jnp.zeros((rest, block.shape[1]), block.dtype))
    return jnp.concatenate(parts, axis=0) if len(parts) > 1 else block


def leaf_factor(work, out, start, base):
    fit = LANES // base
    tile = start // LANES * LANES
    off = start - tile
    lane = lax.broadcasted_iota(jnp.int32, (base, LANES), 1)
    row = lax.broadcasted_iota(jnp.int32, (base, LANES), 0)
    col = lane % base
    seg = lane // base
    groups = [range(g, min(g + fit, len(work))) for g in range(0, len(work), fit)]
    packs, pivots = [], []
    for group in groups:
        packed = jnp.where(col == row, 1.0, 0.0)
        for k in group:
            block = work[k][start:start + base, tile:tile + LANES]
            shift = (base * (k % fit) - off) % LANES
            if shift:
                block = pltpu.roll(block, shift, 1)
            packed = jnp.where(seg == k % fit, block, packed)
        packs.append(packed)
        pivots.append(jnp.ones((base, LANES), jnp.float32))
    for first in range(0, base, WIDE):
        low = first // 8 * 8
        rows = row[low:]
        cols = col[low:]
        for g in range(len(groups)):
            active = packs[g][low:]
            columns = [jnp.take_along_axis(active, (seg * base + first + t)[low:], axis=1) for t in range(WIDE)]
            for t in range(WIDE):
                j = first + t
                at = j - low
                pivot = columns[t][at:at + 1, :]
                pivots[g] = jnp.where(row == j, pivot, pivots[g])
                if j == base - 1:
                    break
                mult = jnp.where(rows > j, columns[t] * (1.0 / pivot), 0.0)
                for s in range(t + 1, WIDE):
                    columns[s] = columns[s] - mult * columns[s][at:at + 1, :]
                pivot_row = jnp.where(col[:1] == j, 1.0, active[at:at + 1, :])
                kept = jnp.where((rows > j) & (cols == j), 0.0, active)
                active = kept - mult * pivot_row
            packs[g] = active if low == 0 else jnp.concatenate([packs[g][:low], active], axis=0)
    inside = (lane >= off) & (lane < off + base)
    for g, group in enumerate(groups):
        unit = jnp.where(col < row, packs[g], jnp.where(col == row, 1.0, 0.0))
        unit = unit * lax.rsqrt(pivots[g])
        for k in group:
            shift = (off - base * (k % fit)) % LANES
            block = pltpu.roll(unit, shift, 1) if shift else unit
            out[k][start:start + base, tile:tile + LANES] = jnp.where(inside, block, 0.0)


def node_factor(work, out, start, size, base):
    if size == base:
        leaf_factor(work, out, start, base)
        return
    half = size // 2
    mid = start + half
    end = start + size
    node_factor(work, out, start, half, base)
    t1 = start // LANES * LANES
    t2 = mid // LANES * LANES
    width = max(LANES, half)
    kept = []
    for k in range(len(work)):
        x1 = out[k][start:mid, t1 : t1 + width]
        l21 = dot3(work[k][mid:end, t1 : t1 + width], x1, NT)
        work[k][mid:end, t2 : t2 + width] -= dot3(l21, pad_rows(l21, mid - t2, width), NT)
        kept.append(dot3(l21, x1, NN))
    node_factor(work, out, mid, half, base)
    for k in range(len(work)):
        x2 = out[k][mid:end, t2 : t2 + width]
        m21 = dot3(x2, pad_rows(kept[k], mid - t2, width), NN)
        out[k][mid:end, t1 : t1 + width] = x2 - m21 if t1 == t2 else -m21


def inverse_kernel(size, core_ref, gram_ref, mine_ref, other_ref, *refs):
    count = mine_ref.shape[0] + 1
    out, work = refs[:count], refs[count:]
    width = mine_ref.shape[2]
    swap = core_ref[0] == 1
    for k in range(count):
        if k == 0:
            work[k][...] = gram_ref[...]
        elif width == size:
            work[k][...] = mine_ref[k - 1]
        else:
            mine, other = mine_ref[k - 1], other_ref[k - 1]
            work[k][:, :width] = jnp.where(swap, other, mine)
            work[k][:, width:] = jnp.where(swap, mine, other)
        for t in range(0, size, LANES):
            out[k][:, t : t + LANES] = jnp.zeros((size, LANES), jnp.float32)
    node_factor(work, out, 0, size, BASE)


def factor_inverse(core, gram, mine, other):
    count, size = mine.shape[0] + 1, gram.shape[0]
    vmem = pl.BlockSpec(memory_space=pltpu.VMEM)
    smem = pl.BlockSpec(memory_space=pltpu.SMEM)
    return pl.pallas_call(
        functools.partial(inverse_kernel, size),
        out_shape=[jax.ShapeDtypeStruct((size, size), jnp.float32)] * count,
        in_specs=[smem, vmem, vmem, vmem],
        out_specs=[vmem] * count,
        scratch_shapes=[pltpu.VMEM((size, size), jnp.float32)] * count,
        cost_estimate=pl.CostEstimate(flops=15 * 10**9, bytes_accessed=8 * count * size**2, transcendentals=0),
        name="factor_inverse",
    )(core, gram, mine, other)


def near_kernel(groups, first_slot, spots, sketched, index_ref, count_ref, blocks_ref, base_ref, *refs):
    pieces = refs[:groups]
    sketch_ref = refs[groups] if sketched else None
    rest = refs[groups + sketched :]
    out_ref = rest[0]
    ext, sems = rest[-2:]
    block_count, slot_count, size, _ = blocks_ref.shape
    copies = []
    at = 0
    for g in range(groups):
        depth = pieces[g].shape[0]
        copies.append(pltpu.make_async_copy(pieces[g], ext.at[pl.ds(at, depth)], sems.at[g]))
        at += depth
    for copy in copies:
        copy.start()
    out_ref[...] = base_ref[...]
    for copy in copies:
        copy.wait()
    for b in range(block_count):
        rows = pl.ds(b * size, size)
        for j in range(first_slot, slot_count):
            spot = index_ref[b, j]
            start = jnp.int32(0)
            here = jnp.bool_(False)
            for order, name in enumerate(spots):
                same = spot == name
                start = jnp.where(same, order * size, start)
                here = here | same

            @pl.when(here & (j < count_ref[b]))
            def _(b=b, j=j, rows=rows, start=start):
                piece = ext[pl.ds(pl.multiple_of(start, size), size), :]
                out_ref[rows, :] -= dot3(blocks_ref[b, j], piece, NN)

    if sketched:
        rest[1][...] = dot3(out_ref[...], sketch_ref[...], NN)


def near_step(blocks, base, pieces, spots, index, count, first_slot, sketch=None):
    block_count, slot_count, size, _ = blocks.shape
    rows, width = base.shape
    total = sum(piece.shape[0] for piece in pieces)
    vmem = pl.BlockSpec(memory_space=pltpu.VMEM)
    smem = pl.BlockSpec(memory_space=pltpu.SMEM)
    hbm = pl.BlockSpec(memory_space=pl.ANY)
    extra = [] if sketch is None else [sketch]
    shapes = [(rows, width)] + [(rows, value.shape[1]) for value in extra]
    return pl.pallas_call(
        functools.partial(near_kernel, len(pieces), first_slot, tuple(spots), len(extra)),
        out_shape=[jax.ShapeDtypeStruct(shape, jnp.float32) for shape in shapes],
        in_specs=[smem, smem, vmem, vmem] + [hbm] * len(pieces) + [vmem] * len(extra),
        out_specs=[vmem] * len(shapes),
        scratch_shapes=[
            pltpu.VMEM((total, width), jnp.float32),
            pltpu.SemaphoreType.DMA((len(pieces),)),
        ],
        cost_estimate=pl.CostEstimate(
            flops=6 * block_count * slot_count * size * size * width,
            bytes_accessed=4 * (total * width + 2 * rows * width + blocks.size),
            transcendentals=0,
        ),
        name="near_step",
    )(index, count, blocks, base, *pieces, *extra)


def leaf_kernel(flag_ref, half_ref, other_ref, far_ref, sketch_ref, gram_ref, part_ref, keep_ref, send_ref, product):
    sketch = half_ref[...] + other_ref[...] if other_ref is not None else half_ref[...]
    sketch_ref[...] = sketch
    turned = sketch.T
    gram = dot3(turned, sketch, NN)
    gram_ref[...] = gram
    rank = gram.shape[0]
    width = part_ref.shape[1]
    part_ref[...] = jnp.where(flag_ref[0] == 1, gram[:, rank - width :], gram[:, :width])
    product[...] = dot3(turned, far_ref[...], NN)
    depth = keep_ref.shape[0]
    keep_ref[...] = product[pl.ds(pl.multiple_of(flag_ref[1], depth), depth), :]
    send_ref[...] = product[pl.ds(pl.multiple_of(flag_ref[2], depth), depth), :]


def leaf_products(flag, part, other, far):
    rows, rank = part.shape
    width = far.shape[1]
    vmem = pl.BlockSpec(memory_space=pltpu.VMEM)
    smem = pl.BlockSpec(memory_space=pltpu.SMEM)
    half = rank // 2
    shapes = [(rows, rank), (rank, rank), (rank, rank if other is None else half), (half, width), (half, width)]
    kernel = leaf_kernel
    args = [flag, part, other, far]
    if other is None:
        args = [flag, part, far]

        def kernel(flag_ref, part_ref, far_ref, *refs):
            leaf_kernel(flag_ref, part_ref, None, far_ref, *refs)

    return pl.pallas_call(
        kernel,
        out_shape=[jax.ShapeDtypeStruct(shape, jnp.float32) for shape in shapes],
        in_specs=[smem] + [vmem] * (len(args) - 1),
        out_specs=[vmem] * len(shapes),
        scratch_shapes=[pltpu.VMEM((rank, width), jnp.float32)],
        cost_estimate=pl.CostEstimate(
            flops=6 * rows * rank * (rank + width), bytes_accessed=4 * rows * (3 * rank + width), transcendentals=0
        ),
        name="leaf_products",
    )(*args)


def reduce_kernel(place_ref, *refs):
    count = LEVELS
    inverses, first, first_other = refs[:count], refs[count], refs[count + 1]
    early, last = refs[count + 2 : count + 6], refs[count + 6 : count + 10]
    out_ref, stage = refs[count + 10 :]
    rank = inverses[0].shape[0]
    half, quarter = rank // 2, rank // 4
    for h in range(count):
        if h == 0:
            parts = [(half, first[...], 0), (half, first_other[...], 1)]
        elif h < count - 1:
            parts = [(quarter, early[i][h - 1], 2 + i) for i in range(4)]
        else:
            parts = [(quarter, last[i][...], 2 + i) for i in range(4)]
        for depth, value, at in parts:
            stage[h, pl.ds(pl.multiple_of(place_ref[at], depth), depth), :] = value
    for h in range(count):
        out_ref[h, 0] = dot3(inverses[h][...], stage[h], NN)


def reduce_all(place, inverses, first, early, last):
    rank, width = inverses[0].shape[0], last[0].shape[1]
    vmem = pl.BlockSpec(memory_space=pltpu.VMEM)
    smem = pl.BlockSpec(memory_space=pltpu.SMEM)
    args = [*inverses, *first, *early, *last]
    return pl.pallas_call(
        reduce_kernel,
        out_shape=jax.ShapeDtypeStruct((LEVELS, 1, rank, width), jnp.float32),
        in_specs=[smem] + [vmem] * len(args),
        out_specs=vmem,
        scratch_shapes=[pltpu.VMEM((LEVELS, rank, width), jnp.float32)],
        cost_estimate=pl.CostEstimate(
            flops=6 * LEVELS * rank * rank * width, bytes_accessed=8 * LEVELS * rank * (rank + width), transcendentals=0
        ),
        name="reduce_all",
    )(place, *args)


def across(value, axis, bit):
    return lax.ppermute(value, axis, [(i, i ^ 1 << bit) for i in range(lax.axis_size(axis))])


def relayed(value, axis):
    count = lax.axis_size(axis)
    steps = [(i, i + 2 if i % 2 == 0 else i - 2) for i in range(count)]
    return lax.ppermute(value, axis, [(i, t) for i, t in steps if 0 <= t < count])


def pick(flag, first, second):
    return jnp.where(flag, second, first)


def halves_of(value, bit):
    half = value.shape[0] // 2
    return pick(bit, value[:half], value[half:]), pick(bit, value[half:], value[:half])


def leaf_and_levels(samples, probes, near_blocks, near_cols, near_count, sketch):
    rows_dev, _ = samples.shape
    block_size = near_blocks.shape[2]
    block_count = rows_dev // block_size
    rank = sketch.shape[1]
    position = lax.axis_index("rows")
    bits = [position >> h & 1 for h in range(LEVELS)]
    odd = bits[0] == 1
    upper = bits[1] == 1
    halves = 2 if lax.axis_size("samp") == 2 else 1
    core = lax.axis_index("samp") % 2
    core_flag = core.reshape(1).astype(jnp.int32)

    index = near_cols - (position * block_count - block_count)
    moved = jnp.where(index < block_count, 2 * block_count, jnp.where(index >= 2 * block_count, -2 * block_count, 0))
    index = index + jnp.where(odd, moved, 0)

    parts = block_count * SPLIT
    depth = rows_dev // parts
    later = lax.optimization_barrier(probes)
    pieces = [(later if i else probes)[i * depth : (i + 1) * depth] for i in range(parts)]
    peer = [across(pieces[i], "rows", 0) for i in range(parts)]
    far = [relayed(peer[i], "rows") for i in range(parts)]

    own = range(block_count, 2 * block_count)
    (left,) = near_step(near_blocks, samples, [probes], own, index, near_count, 0)
    early = (block_count - 1) * SPLIT
    spots = [*range(block_count - 1), *range(2 * block_count, 3 * block_count)]
    (left,) = near_step(near_blocks, left, far[:early] + peer, spots, index, near_count, 1)
    far_samples, partial = near_step(near_blocks, left, far[early:], [block_count - 1], index, near_count, 1, sketch)
    if halves == 2:
        other = across(partial, "samp", 0)
    else:
        partial, other = lax.psum(partial, "samp"), None
    flag = jnp.stack([core, bits[0] * (rank // 2), (1 - bits[0]) * (rank // 2)]).astype(jnp.int32)
    leaf_sketch, gram, part, keep, send = leaf_products(flag, partial, other, far_samples)

    sums = []
    for h in range(LEVELS):
        part = part + across(part, "rows", h)
        sums.append(part)
    sums = jnp.stack(sums)
    sums_other = across(sums, "samp", 0) if halves == 2 else sums
    leaf_inverse, *inverses = factor_inverse(core_flag, gram, sums, sums_other)
    leaf_basis = lax.dot_general(leaf_sketch, leaf_inverse, (NT, ((), ())), precision=HIGH)

    first = keep + across(send, "rows", 0)
    first_other = across(first, "rows", 0)
    keep, send = halves_of(first, upper)
    quarter = keep + across(send, "rows", 1)
    quarters = [quarter]
    for h in range(2, LEVELS):
        quarter = quarter + across(quarter, "rows", h)
        quarters.append(quarter)

    def gathered(value):
        along = across(value, "rows", 1)
        beside = across(value, "rows", 0)
        diagonal = across(along, "rows", 0)
        return [value, along, beside, diagonal]

    early = gathered(jnp.stack(quarters[:-1]))
    last = gathered(quarters[-1])
    half = rank // 2
    x, y = bits[0] * half, bits[1] * (half // 2)
    fx, fy = half - x, half // 2 - y
    place = jnp.stack([x, fx, x + y, x + fy, fx + y, fx + fy]).astype(jnp.int32)
    reduced = reduce_all(place, inverses, [first, first_other], early, last)
    return (leaf_basis, reduced)


def solution(mesh):
    return jax.shard_map(
        leaf_and_levels,
        mesh=mesh,
        in_specs=(
            P("rows", "samp"),
            P("rows", "samp"),
            P("rows", None, None, None),
            P("rows", None),
            P("rows"),
            P("samp", None),
        ),
        out_specs=(P("rows", None), P(None, "rows", None, "samp")),
        check_vma=False,
    )
```

```python
import functools

import jax
import jax.numpy as jnp
from jax import lax
from jax.experimental import pallas as pl
from jax.experimental.pallas import tpu as pltpu
from jax.sharding import PartitionSpec as P

LEVELS = 4
LANES = 128
BASE = 64
WIDE = 16
SPLIT = 2
NN = ((1,), (0,))
NT = ((1,), (1,))
HIGH = lax.Precision.HIGH


def split(value):
    high = value.astype(jnp.bfloat16)
    return high, (value - high.astype(jnp.float32)).astype(jnp.bfloat16)


def dot3(left, right, dims):
    lh, ll = split(left)
    rh, rl = split(right)

    def product(a, b):
        return lax.dot_general(a, b, (dims, ((), ())), preferred_element_type=jnp.float32)

    return product(lh, rh) + (product(lh, rl) + product(ll, rh))


def pad_rows(block, start, total):
    parts = []
    if start:
        parts.append(jnp.zeros((start, block.shape[1]), block.dtype))
    parts.append(block)
    rest = total - start - block.shape[0]
    if rest:
        parts.append(jnp.zeros((rest, block.shape[1]), block.dtype))
    return jnp.concatenate(parts, axis=0) if len(parts) > 1 else block


def leaf_factor(work, out, start, base):
    fit = LANES // base
    tile = start // LANES * LANES
    off = start - tile
    lane = lax.broadcasted_iota(jnp.int32, (base, LANES), 1)
    row = lax.broadcasted_iota(jnp.int32, (base, LANES), 0)
    col = lane % base
    seg = lane // base
    groups = [range(g, min(g + fit, len(work))) for g in range(0, len(work), fit)]
    packs, pivots = [], []
    for group in groups:
        packed = jnp.where(col == row, 1.0, 0.0)
        for k in group:
            block = work[k][start:start + base, tile:tile + LANES]
            shift = (base * (k % fit) - off) % LANES
            if shift:
                block = pltpu.roll(block, shift, 1)
            packed = jnp.where(seg == k % fit, block, packed)
        packs.append(packed)
        pivots.append(jnp.ones((base, LANES), jnp.float32))
    for first in range(0, base, WIDE):
        low = first // 8 * 8
        rows = row[low:]
        cols = col[low:]
        for g in range(len(groups)):
            active = packs[g][low:]
            columns = [jnp.take_along_axis(active, (seg * base + first + t)[low:], axis=1) for t in range(WIDE)]
            for t in range(WIDE):
                j = first + t
                at = j - low
                pivot = columns[t][at:at + 1, :]
                pivots[g] = jnp.where(row == j, pivot, pivots[g])
                if j == base - 1:
                    break
                mult = jnp.where(rows > j, columns[t] * (1.0 / pivot), 0.0)
                for s in range(t + 1, WIDE):
                    columns[s] = columns[s] - mult * columns[s][at:at + 1, :]
                pivot_row = jnp.where(col[:1] == j, 1.0, active[at:at + 1, :])
                kept = jnp.where((rows > j) & (cols == j), 0.0, active)
                active = kept - mult * pivot_row
            packs[g] = active if low == 0 else jnp.concatenate([packs[g][:low], active], axis=0)
    inside = (lane >= off) & (lane < off + base)
    for g, group in enumerate(groups):
        unit = jnp.where(col < row, packs[g], jnp.where(col == row, 1.0, 0.0))
        unit = unit * lax.rsqrt(pivots[g])
        for k in group:
            shift = (off - base * (k % fit)) % LANES
            block = pltpu.roll(unit, shift, 1) if shift else unit
            out[k][start:start + base, tile:tile + LANES] = jnp.where(inside, block, 0.0)


def node_factor(work, out, start, size, base):
    if size == base:
        leaf_factor(work, out, start, base)
        return
    half = size // 2
    mid = start + half
    end = start + size
    node_factor(work, out, start, half, base)
    t1 = start // LANES * LANES
    t2 = mid // LANES * LANES
    width = max(LANES, half)
    kept = []
    for k in range(len(work)):
        x1 = out[k][start:mid, t1 : t1 + width]
        l21 = dot3(work[k][mid:end, t1 : t1 + width], x1, NT)
        work[k][mid:end, t2 : t2 + width] -= dot3(l21, pad_rows(l21, mid - t2, width), NT)
        kept.append(dot3(l21, x1, NN))
    node_factor(work, out, mid, half, base)
    for k in range(len(work)):
        x2 = out[k][mid:end, t2 : t2 + width]
        m21 = dot3(x2, pad_rows(kept[k], mid - t2, width), NN)
        out[k][mid:end, t1 : t1 + width] = x2 - m21 if t1 == t2 else -m21


def inverse_kernel(size, core_ref, gram_ref, mine_ref, other_ref, *refs):
    count = mine_ref.shape[0] + 1
    out, work = refs[:count], refs[count:]
    width = mine_ref.shape[2]
    swap = core_ref[0] == 1
    for k in range(count):
        if k == 0:
            work[k][...] = gram_ref[...]
        elif width == size:
            work[k][...] = mine_ref[k - 1]
        else:
            mine, other = mine_ref[k - 1], other_ref[k - 1]
            work[k][:, :width] = jnp.where(swap, other, mine)
            work[k][:, width:] = jnp.where(swap, mine, other)
        for t in range(0, size, LANES):
            out[k][:, t : t + LANES] = jnp.zeros((size, LANES), jnp.float32)
    node_factor(work, out, 0, size, BASE)


def factor_inverse(core, gram, mine, other):
    count, size = mine.shape[0] + 1, gram.shape[0]
    vmem = pl.BlockSpec(memory_space=pltpu.VMEM)
    smem = pl.BlockSpec(memory_space=pltpu.SMEM)
    return pl.pallas_call(
        functools.partial(inverse_kernel, size),
        out_shape=[pltpu.VMEM((size, size), jnp.float32)] * count,
        in_specs=[smem, vmem, vmem, vmem],
        out_specs=[vmem] * count,
        scratch_shapes=[pltpu.VMEM((size, size), jnp.float32)] * count,
        cost_estimate=pl.CostEstimate(flops=15 * 10**9, bytes_accessed=8 * count * size**2, transcendentals=0),
        name="factor_inverse",
    )(core, gram, mine, other)


def near_kernel(groups, first_slot, spots, sketched, index_ref, count_ref, blocks_ref, base_ref, *refs):
    pieces = refs[:groups]
    sketch_ref = refs[groups] if sketched else None
    rest = refs[groups + sketched :]
    out_ref = rest[0]
    ext, sems = rest[-2:]
    block_count, slot_count, size, _ = blocks_ref.shape
    copies = []
    at = 0
    for g in range(groups):
        depth = pieces[g].shape[0]
        copies.append(pltpu.make_async_copy(pieces[g], ext.at[pl.ds(at, depth)], sems.at[g]))
        at += depth
    for copy in copies:
        copy.start()
    out_ref[...] = base_ref[...]
    for copy in copies:
        copy.wait()
    for b in range(block_count):
        rows = pl.ds(b * size, size)
        for j in range(first_slot, slot_count):
            spot = index_ref[b, j]
            start = jnp.int32(0)
            here = jnp.bool_(False)
            for order, name in enumerate(spots):
                same = spot == name
                start = jnp.where(same, order * size, start)
                here = here | same

            @pl.when(here & (j < count_ref[b]))
            def _(b=b, j=j, rows=rows, start=start):
                piece = ext[pl.ds(pl.multiple_of(start, size), size), :]
                out_ref[rows, :] -= dot3(blocks_ref[b, j], piece, NN)

    if sketched:
        rest[1][...] = dot3(out_ref[...], sketch_ref[...], NN)


def near_step(blocks, base, pieces, spots, index, count, first_slot, sketch=None):
    block_count, slot_count, size, _ = blocks.shape
    rows, width = base.shape
    total = sum(piece.shape[0] for piece in pieces)
    vmem = pl.BlockSpec(memory_space=pltpu.VMEM)
    smem = pl.BlockSpec(memory_space=pltpu.SMEM)
    hbm = pl.BlockSpec(memory_space=pl.ANY)
    extra = [] if sketch is None else [sketch]
    shapes = [(rows, width)] + [(rows, value.shape[1]) for value in extra]
    return pl.pallas_call(
        functools.partial(near_kernel, len(pieces), first_slot, tuple(spots), len(extra)),
        out_shape=[pltpu.VMEM(shape, jnp.float32) for shape in shapes],
        in_specs=[smem, smem, vmem, vmem] + [hbm] * len(pieces) + [vmem] * len(extra),
        out_specs=[vmem] * len(shapes),
        scratch_shapes=[
            pltpu.VMEM((total, width), jnp.float32),
            pltpu.SemaphoreType.DMA((len(pieces),)),
        ],
        cost_estimate=pl.CostEstimate(
            flops=6 * block_count * slot_count * size * size * width,
            bytes_accessed=4 * (total * width + 2 * rows * width + blocks.size),
            transcendentals=0,
        ),
        name="near_step",
    )(index, count, blocks, base, *pieces, *extra)


def leaf_kernel(flag_ref, half_ref, other_ref, far_ref, sketch_ref, gram_ref, part_ref, keep_ref, send_ref, product):
    sketch = half_ref[...] + other_ref[...] if other_ref is not None else half_ref[...]
    sketch_ref[...] = sketch
    turned = sketch.T
    gram = dot3(turned, sketch, NN)
    gram_ref[...] = gram
    rank = gram.shape[0]
    width = part_ref.shape[1]
    part_ref[...] = jnp.where(flag_ref[0] == 1, gram[:, rank - width :], gram[:, :width])
    product[...] = dot3(turned, far_ref[...], NN)
    depth = keep_ref.shape[0]
    keep_ref[...] = product[pl.ds(pl.multiple_of(flag_ref[1], depth), depth), :]
    send_ref[...] = product[pl.ds(pl.multiple_of(flag_ref[2], depth), depth), :]


def leaf_products(flag, part, other, far):
    rows, rank = part.shape
    width = far.shape[1]
    vmem = pl.BlockSpec(memory_space=pltpu.VMEM)
    smem = pl.BlockSpec(memory_space=pltpu.SMEM)
    half = rank // 2
    shapes = [(rows, rank), (rank, rank), (rank, rank if other is None else half), (half, width), (half, width)]
    kernel = leaf_kernel
    args = [flag, part, other, far]
    if other is None:
        args = [flag, part, far]

        def kernel(flag_ref, part_ref, far_ref, *refs):
            leaf_kernel(flag_ref, part_ref, None, far_ref, *refs)

    return pl.pallas_call(
        kernel,
        out_shape=[pltpu.VMEM(shape, jnp.float32) for shape in shapes],
        in_specs=[smem] + [vmem] * (len(args) - 1),
        out_specs=[vmem] * len(shapes),
        scratch_shapes=[pltpu.VMEM((rank, width), jnp.float32)],
        cost_estimate=pl.CostEstimate(
            flops=6 * rows * rank * (rank + width), bytes_accessed=4 * rows * (3 * rank + width), transcendentals=0
        ),
        name="leaf_products",
    )(*args)


def staged(stage, place_ref, parts):
    for value, at in parts:
        depth = value.shape[0]
        stage[pl.ds(pl.multiple_of(place_ref[at], depth), depth), :] = value
    return stage[...]


def early_kernel(place_ref, *refs):
    count = LEVELS - 1
    inverses, first = refs[:count], refs[count : count + 2]
    early = refs[count + 2 : count + 6]
    out_ref, stage, result, sems = refs[count + 6 :]
    copies = []
    for h in range(count):
        if h == 0:
            parts = [(first[0][...], 0), (first[1][...], 1)]
        else:
            parts = [(early[i][h - 1], 2 + i) for i in range(4)]
        result[h] = dot3(inverses[h][...], staged(stage.at[h], place_ref, parts), NN)
        copies.append(pltpu.make_async_copy(result.at[h], out_ref.at[h, 0], sems.at[h]))
        copies[-1].start()
    for copy in copies:
        copy.wait()


def reduce_early(place, inverses, first, early):
    rank, width = inverses[0].shape[0], first[0].shape[1]
    vmem = pl.BlockSpec(memory_space=pltpu.VMEM)
    smem = pl.BlockSpec(memory_space=pltpu.SMEM)
    args = [*inverses, *first, *early]
    count = LEVELS - 1
    return pl.pallas_call(
        early_kernel,
        out_shape=jax.ShapeDtypeStruct((LEVELS, 1, rank, width), jnp.float32),
        in_specs=[smem] + [vmem] * len(args),
        out_specs=pl.BlockSpec(memory_space=pl.ANY),
        scratch_shapes=[
            pltpu.VMEM((count, rank, width), jnp.float32),
            pltpu.VMEM((count, rank, width), jnp.float32),
            pltpu.SemaphoreType.DMA((count,)),
        ],
        cost_estimate=pl.CostEstimate(
            flops=6 * count * rank * rank * width, bytes_accessed=8 * count * rank * (rank + width), transcendentals=0
        ),
        name="reduce_early",
    )(place, *args)


def last_kernel(place_ref, inverse_ref, *refs):
    last = refs[:4]
    out_ref, stage, result, sem = refs[5:]
    value = staged(stage, place_ref, [(last[i][...], 2 + i) for i in range(4)])
    result[...] = dot3(inverse_ref[...], value, NN)
    copy = pltpu.make_async_copy(result, out_ref.at[LEVELS - 1, 0], sem)
    copy.start()
    copy.wait()


def reduce_last(place, inverse, last, reduced):
    rank, width = inverse.shape[0], last[0].shape[1]
    vmem = pl.BlockSpec(memory_space=pltpu.VMEM)
    smem = pl.BlockSpec(memory_space=pltpu.SMEM)
    hbm = pl.BlockSpec(memory_space=pl.ANY)
    return pl.pallas_call(
        last_kernel,
        out_shape=jax.ShapeDtypeStruct(reduced.shape, jnp.float32),
        in_specs=[smem] + [vmem] * 5 + [hbm],
        out_specs=hbm,
        scratch_shapes=[
            pltpu.VMEM((rank, width), jnp.float32),
            pltpu.VMEM((rank, width), jnp.float32),
            pltpu.SemaphoreType.DMA,
        ],
        input_output_aliases={6: 0},
        cost_estimate=pl.CostEstimate(
            flops=6 * rank * rank * width, bytes_accessed=8 * rank * (rank + width), transcendentals=0
        ),
        name="reduce_last",
    )(place, inverse, *last, reduced)


def across(value, axis, bit):
    return lax.ppermute(value, axis, [(i, i ^ 1 << bit) for i in range(lax.axis_size(axis))])


def diagonal_of(value, axis):
    return lax.ppermute(value, axis, [(i, i ^ 3) for i in range(lax.axis_size(axis))])


def relayed(value, axis):
    count = lax.axis_size(axis)
    steps = [(i, i + 2 if i % 2 == 0 else i - 2) for i in range(count)]
    return lax.ppermute(value, axis, [(i, t) for i, t in steps if 0 <= t < count])


def pick(flag, first, second):
    return jnp.where(flag, second, first)


def halves_of(value, bit):
    half = value.shape[0] // 2
    return pick(bit, value[:half], value[half:]), pick(bit, value[half:], value[:half])


def leaf_and_levels(samples, probes, near_blocks, near_cols, near_count, sketch):
    rows_dev, _ = samples.shape
    block_size = near_blocks.shape[2]
    block_count = rows_dev // block_size
    rank = sketch.shape[1]
    position = lax.axis_index("rows")
    bits = [position >> h & 1 for h in range(LEVELS)]
    odd = bits[0] == 1
    upper = bits[1] == 1
    halves = 2 if lax.axis_size("samp") == 2 else 1
    core = lax.axis_index("samp") % 2
    core_flag = core.reshape(1).astype(jnp.int32)

    index = near_cols - (position * block_count - block_count)
    moved = jnp.where(index < block_count, 2 * block_count, jnp.where(index >= 2 * block_count, -2 * block_count, 0))
    index = index + jnp.where(odd, moved, 0)

    parts = block_count * SPLIT
    depth = rows_dev // parts
    later = lax.optimization_barrier(probes)
    pieces = [(later if i else probes)[i * depth : (i + 1) * depth] for i in range(parts)]
    peer = [across(pieces[i], "rows", 0) for i in range(parts)]
    far = [relayed(peer[i], "rows") for i in range(parts)]

    own = range(block_count, 2 * block_count)
    (left,) = near_step(near_blocks, samples, [probes], own, index, near_count, 0)
    early = (block_count - 1) * SPLIT
    spots = [*range(block_count - 1), *range(2 * block_count, 3 * block_count)]
    (left,) = near_step(near_blocks, left, far[:early] + peer, spots, index, near_count, 1)
    far_samples, partial = near_step(near_blocks, left, far[early:], [block_count - 1], index, near_count, 1, sketch)
    if halves == 2:
        other = across(partial, "samp", 0)
    else:
        partial, other = lax.psum(partial, "samp"), None
    flag = jnp.stack([core, bits[0] * (rank // 2), (1 - bits[0]) * (rank // 2)]).astype(jnp.int32)
    leaf_sketch, gram, part, keep, send = leaf_products(flag, partial, other, far_samples)

    sums = []
    for h in range(LEVELS):
        part = part + across(part, "rows", h)
        sums.append(part)
    sums = jnp.stack(sums)
    sums_other = across(sums, "samp", 0) if halves == 2 else sums
    leaf_inverse, *inverses = factor_inverse(core_flag, gram, sums, sums_other)
    leaf_basis = lax.dot_general(leaf_sketch, leaf_inverse, (NT, ((), ())), precision=HIGH)

    first = keep + across(send, "rows", 0)
    first_other = across(first, "rows", 0)
    keep, send = halves_of(first, upper)
    quarter = keep + across(send, "rows", 1)
    quarters = [quarter]
    for h in range(2, LEVELS):
        quarter = quarter + across(quarter, "rows", h)
        quarters.append(quarter)

    def gathered(value):
        along = across(value, "rows", 1)
        beside = across(value, "rows", 0)
        diagonal = diagonal_of(value, "rows")
        return [value, along, beside, diagonal]

    early = gathered(jnp.stack(quarters[:-1]))
    last = gathered(quarters[-1])
    half = rank // 2
    x, y = bits[0] * half, bits[1] * (half // 2)
    fx, fy = half - x, half // 2 - y
    place = jnp.stack([x, fx, x + y, x + fy, fx + y, fx + fy]).astype(jnp.int32)
    reduced = reduce_early(place, inverses[:-1], [first, first_other], early)
    reduced = reduce_last(place, inverses[-1], last, reduced)
    return (leaf_basis, reduced)


def solution(mesh):
    return jax.shard_map(
        leaf_and_levels,
        mesh=mesh,
        in_specs=(
            P("rows", "samp"),
            P("rows", "samp"),
            P("rows", None, None, None),
            P("rows", None),
            P("rows"),
            P("samp", None),
        ),
        out_specs=(P("rows", None), P(None, "rows", None, "samp")),
        check_vma=False,
    )
```

```python
import functools

import jax
import jax.numpy as jnp
from jax import lax
from jax.experimental import pallas as pl
from jax.experimental.pallas import tpu as pltpu
from jax.sharding import PartitionSpec as P

LEVELS = 4
LANES = 128
BASE = 64
WIDE = 16
SPLIT = 2
NN = ((1,), (0,))
NT = ((1,), (1,))
HIGH = lax.Precision.HIGH


def split(value):
    high = value.astype(jnp.bfloat16)
    return high, (value - high.astype(jnp.float32)).astype(jnp.bfloat16)


def dot3(left, right, dims):
    lh, ll = split(left)
    rh, rl = split(right)

    def product(a, b):
        return lax.dot_general(a, b, (dims, ((), ())), preferred_element_type=jnp.float32)

    return product(lh, rh) + (product(lh, rl) + product(ll, rh))


def pad_rows(block, start, total):
    parts = []
    if start:
        parts.append(jnp.zeros((start, block.shape[1]), block.dtype))
    parts.append(block)
    rest = total - start - block.shape[0]
    if rest:
        parts.append(jnp.zeros((rest, block.shape[1]), block.dtype))
    return jnp.concatenate(parts, axis=0) if len(parts) > 1 else block


def leaf_factor(work, out, start, base):
    fit = LANES // base
    tile = start // LANES * LANES
    off = start - tile
    lane = lax.broadcasted_iota(jnp.int32, (base, LANES), 1)
    row = lax.broadcasted_iota(jnp.int32, (base, LANES), 0)
    col = lane % base
    seg = lane // base
    groups = [range(g, min(g + fit, len(work))) for g in range(0, len(work), fit)]
    packs, pivots = [], []
    for group in groups:
        packed = jnp.where(col == row, 1.0, 0.0)
        for k in group:
            block = work[k][start:start + base, tile:tile + LANES]
            shift = (base * (k % fit) - off) % LANES
            if shift:
                block = pltpu.roll(block, shift, 1)
            packed = jnp.where(seg == k % fit, block, packed)
        packs.append(packed)
        pivots.append(jnp.ones((base, LANES), jnp.float32))
    for first in range(0, base, WIDE):
        low = first // 8 * 8
        rows = row[low:]
        cols = col[low:]
        for g in range(len(groups)):
            active = packs[g][low:]
            columns = [jnp.take_along_axis(active, (seg * base + first + t)[low:], axis=1) for t in range(WIDE)]
            for t in range(WIDE):
                j = first + t
                at = j - low
                pivot = columns[t][at:at + 1, :]
                pivots[g] = jnp.where(row == j, pivot, pivots[g])
                if j == base - 1:
                    break
                mult = jnp.where(rows > j, columns[t] * (1.0 / pivot), 0.0)
                for s in range(t + 1, WIDE):
                    columns[s] = columns[s] - mult * columns[s][at:at + 1, :]
                pivot_row = jnp.where(col[:1] == j, 1.0, active[at:at + 1, :])
                kept = jnp.where((rows > j) & (cols == j), 0.0, active)
                active = kept - mult * pivot_row
            packs[g] = active if low == 0 else jnp.concatenate([packs[g][:low], active], axis=0)
    inside = (lane >= off) & (lane < off + base)
    for g, group in enumerate(groups):
        unit = jnp.where(col < row, packs[g], jnp.where(col == row, 1.0, 0.0))
        unit = unit * lax.rsqrt(pivots[g])
        for k in group:
            shift = (off - base * (k % fit)) % LANES
            block = pltpu.roll(unit, shift, 1) if shift else unit
            out[k][start:start + base, tile:tile + LANES] = jnp.where(inside, block, 0.0)


def node_factor(work, out, start, size, base):
    if size == base:
        leaf_factor(work, out, start, base)
        return
    half = size // 2
    mid = start + half
    end = start + size
    node_factor(work, out, start, half, base)
    t1 = start // LANES * LANES
    t2 = mid // LANES * LANES
    width = max(LANES, half)
    kept = []
    for k in range(len(work)):
        x1 = out[k][start:mid, t1 : t1 + width]
        l21 = dot3(work[k][mid:end, t1 : t1 + width], x1, NT)
        work[k][mid:end, t2 : t2 + width] -= dot3(l21, pad_rows(l21, mid - t2, width), NT)
        kept.append(dot3(l21, x1, NN))
    node_factor(work, out, mid, half, base)
    for k in range(len(work)):
        x2 = out[k][mid:end, t2 : t2 + width]
        m21 = dot3(x2, pad_rows(kept[k], mid - t2, width), NN)
        out[k][mid:end, t1 : t1 + width] = x2 - m21 if t1 == t2 else -m21


def inverse_kernel(size, core_ref, gram_ref, mine_ref, other_ref, *refs):
    count = mine_ref.shape[0] + 1
    out, work = refs[:count], refs[count:]
    width = mine_ref.shape[2]
    swap = core_ref[0] == 1
    for k in range(count):
        if k == 0:
            work[k][...] = gram_ref[...]
        elif width == size:
            work[k][...] = mine_ref[k - 1]
        else:
            mine, other = mine_ref[k - 1], other_ref[k - 1]
            work[k][:, :width] = jnp.where(swap, other, mine)
            work[k][:, width:] = jnp.where(swap, mine, other)
        for t in range(0, size, LANES):
            out[k][:, t : t + LANES] = jnp.zeros((size, LANES), jnp.float32)
    node_factor(work, out, 0, size, BASE)


def factor_inverse(core, gram, mine, other):
    count, size = mine.shape[0] + 1, gram.shape[0]
    vmem = pl.BlockSpec(memory_space=pltpu.VMEM)
    smem = pl.BlockSpec(memory_space=pltpu.SMEM)
    return pl.pallas_call(
        functools.partial(inverse_kernel, size),
        out_shape=[pltpu.VMEM((size, size), jnp.float32)] * count,
        in_specs=[smem, vmem, vmem, vmem],
        out_specs=[vmem] * count,
        scratch_shapes=[pltpu.VMEM((size, size), jnp.float32)] * count,
        cost_estimate=pl.CostEstimate(flops=15 * 10**9, bytes_accessed=8 * count * size**2, transcendentals=0),
        name="factor_inverse",
    )(core, gram, mine, other)


def near_kernel(groups, first_slot, spots, sketched, index_ref, count_ref, flag_ref, blocks_ref, base_ref, *refs):
    pieces = refs[:groups]
    sketch_ref = refs[groups] if sketched else None
    rest = refs[groups + sketched :]
    out_ref, ext = rest[0], rest[-1]
    block_count, slot_count, size, _ = blocks_ref.shape
    at = 0
    for g in range(groups):
        depth = pieces[g].shape[0]
        ext[at : at + depth, :] = pieces[g][...]
        at += depth
    out_ref[...] = base_ref[...]
    for b in range(block_count):
        rows = pl.ds(b * size, size)
        for j in range(first_slot, slot_count):
            spot = index_ref[b, j]
            start = jnp.int32(0)
            here = jnp.bool_(False)
            for order, name in enumerate(spots):
                same = spot == name
                start = jnp.where(same, order * size, start)
                here = here | same

            @pl.when(here & (j < count_ref[b]))
            def _(b=b, j=j, rows=rows, start=start):
                piece = ext[pl.ds(pl.multiple_of(start, size), size), :]
                out_ref[rows, :] -= dot3(blocks_ref[b, j], piece, NN)

    if sketched:
        rest[1][...] = dot3(out_ref[...], sketch_ref[...], NN)


def near_step(blocks, base, pieces, spots, index, count, flag, first_slot, sketch=None):
    block_count, slot_count, size, _ = blocks.shape
    rows, width = base.shape
    total = sum(piece.shape[0] for piece in pieces)
    vmem = pl.BlockSpec(memory_space=pltpu.VMEM)
    smem = pl.BlockSpec(memory_space=pltpu.SMEM)
    extra = [] if sketch is None else [sketch]
    shapes = [(rows, width)] + [(rows, value.shape[1]) for value in extra]
    return pl.pallas_call(
        functools.partial(near_kernel, len(pieces), first_slot, tuple(spots), len(extra)),
        out_shape=[pltpu.VMEM(shape, jnp.float32) for shape in shapes],
        in_specs=[smem] * 3 + [vmem] * (2 + len(pieces) + len(extra)),
        out_specs=[vmem] * len(shapes),
        scratch_shapes=[pltpu.VMEM((total, width), jnp.float32)],
        cost_estimate=pl.CostEstimate(
            flops=6 * block_count * slot_count * size * size * width,
            bytes_accessed=4 * (total * width + 2 * rows * width + blocks.size),
            transcendentals=0,
        ),
        name="near_step",
    )(index, count, flag, blocks, base, *pieces, *extra)


def leaf_kernel(flag_ref, half_ref, other_ref, far_ref, sketch_ref, gram_ref, part_ref, keep_ref, send_ref, product):
    sketch = half_ref[...] + other_ref[...] if other_ref is not None else half_ref[...]
    sketch_ref[...] = sketch
    turned = sketch.T
    gram = dot3(turned, sketch, NN)
    gram_ref[...] = gram
    rank = gram.shape[0]
    width = part_ref.shape[1]
    part_ref[...] = jnp.where(flag_ref[0] == 1, gram[:, rank - width :], gram[:, :width])
    product[...] = dot3(turned, far_ref[...], NN)
    depth = keep_ref.shape[0]
    keep_ref[...] = product[pl.ds(pl.multiple_of(flag_ref[1], depth), depth), :]
    send_ref[...] = product[pl.ds(pl.multiple_of(flag_ref[2], depth), depth), :]


def leaf_products(flag, part, other, far):
    rows, rank = part.shape
    width = far.shape[1]
    vmem = pl.BlockSpec(memory_space=pltpu.VMEM)
    smem = pl.BlockSpec(memory_space=pltpu.SMEM)
    half = rank // 2
    shapes = [(rows, rank), (rank, rank), (rank, rank if other is None else half), (half, width), (half, width)]
    kernel = leaf_kernel
    args = [flag, part, other, far]
    if other is None:
        args = [flag, part, far]

        def kernel(flag_ref, part_ref, far_ref, *refs):
            leaf_kernel(flag_ref, part_ref, None, far_ref, *refs)

    return pl.pallas_call(
        kernel,
        out_shape=[pltpu.VMEM(shape, jnp.float32) for shape in shapes],
        in_specs=[smem] + [vmem] * (len(args) - 1),
        out_specs=[vmem] * len(shapes),
        scratch_shapes=[pltpu.VMEM((rank, width), jnp.float32)],
        cost_estimate=pl.CostEstimate(
            flops=6 * rows * rank * (rank + width), bytes_accessed=4 * rows * (3 * rank + width), transcendentals=0
        ),
        name="leaf_products",
    )(*args)


def staged(stage, flag_ref, mine, other):
    depth = mine.shape[0]
    stage[pl.ds(pl.multiple_of(flag_ref[1], depth), depth), :] = mine
    stage[pl.ds(pl.multiple_of(flag_ref[2], depth), depth), :] = other
    return stage[...]


def early_kernel(flag_ref, *refs):
    count = LEVELS - 1
    inverses, mine_ref, other_ref = refs[:count], refs[count], refs[count + 1]
    out_ref, stage, result, sems = refs[count + 2 :]
    copies = []
    for h in range(count):
        result[h] = dot3(inverses[h][...], staged(stage.at[h], flag_ref, mine_ref[h], other_ref[h]), NN)
        copies.append(pltpu.make_async_copy(result.at[h], out_ref.at[h, 0], sems.at[h]))
        copies[-1].start()
    for copy in copies:
        copy.wait()


def reduce_early(flag, inverses, mine, other):
    rank, width = inverses[0].shape[0], mine.shape[2]
    vmem = pl.BlockSpec(memory_space=pltpu.VMEM)
    smem = pl.BlockSpec(memory_space=pltpu.SMEM)
    count = LEVELS - 1
    return pl.pallas_call(
        early_kernel,
        out_shape=jax.ShapeDtypeStruct((LEVELS, 1, rank, width), jnp.float32),
        in_specs=[smem] + [vmem] * (count + 2),
        out_specs=pl.BlockSpec(memory_space=pl.ANY),
        scratch_shapes=[
            pltpu.VMEM((count, rank, width), jnp.float32),
            pltpu.VMEM((count, rank, width), jnp.float32),
            pltpu.SemaphoreType.DMA((count,)),
        ],
        cost_estimate=pl.CostEstimate(
            flops=6 * count * rank * rank * width, bytes_accessed=8 * count * rank * (rank + width), transcendentals=0
        ),
        name="reduce_early",
    )(flag, *inverses, mine, other)


def last_kernel(flag_ref, inverse_ref, mine_ref, other_ref, kept_ref, out_ref, stage, result, sem):
    result[...] = dot3(inverse_ref[...], staged(stage, flag_ref, mine_ref[...], other_ref[...]), NN)
    copy = pltpu.make_async_copy(result, out_ref.at[LEVELS - 1, 0], sem)
    copy.start()
    copy.wait()


def reduce_last(flag, inverse, mine, other, reduced):
    rank, width = inverse.shape[0], mine.shape[1]
    vmem = pl.BlockSpec(memory_space=pltpu.VMEM)
    smem = pl.BlockSpec(memory_space=pltpu.SMEM)
    hbm = pl.BlockSpec(memory_space=pl.ANY)
    return pl.pallas_call(
        last_kernel,
        out_shape=jax.ShapeDtypeStruct(reduced.shape, jnp.float32),
        in_specs=[smem] + [vmem] * 3 + [hbm],
        out_specs=hbm,
        scratch_shapes=[
            pltpu.VMEM((rank, width), jnp.float32),
            pltpu.VMEM((rank, width), jnp.float32),
            pltpu.SemaphoreType.DMA,
        ],
        input_output_aliases={4: 0},
        cost_estimate=pl.CostEstimate(
            flops=6 * rank * rank * width, bytes_accessed=8 * rank * (rank + width), transcendentals=0
        ),
        name="reduce_last",
    )(flag, inverse, mine, other, reduced)


def across(value, axis, bit):
    return lax.ppermute(value, axis, [(i, i ^ 1 << bit) for i in range(lax.axis_size(axis))])


def relayed(value, axis):
    count = lax.axis_size(axis)
    steps = [(i, i + 2 if i % 2 == 0 else i - 2) for i in range(count)]
    return lax.ppermute(value, axis, [(i, t) for i, t in steps if 0 <= t < count])


def leaf_and_levels(samples, probes, near_blocks, near_cols, near_count, sketch):
    rows_dev, _ = samples.shape
    block_size = near_blocks.shape[2]
    block_count = rows_dev // block_size
    rank = sketch.shape[1]
    position = lax.axis_index("rows")
    bits = [position >> h & 1 for h in range(LEVELS)]
    odd = bits[0] == 1
    halves = 2 if lax.axis_size("samp") == 2 else 1
    core = lax.axis_index("samp") % 2
    half = rank // 2
    flag = jnp.stack([core, bits[0] * half, half - bits[0] * half]).astype(jnp.int32)

    index = near_cols - (position * block_count - block_count)
    moved = jnp.where(index < block_count, 2 * block_count, jnp.where(index >= 2 * block_count, -2 * block_count, 0))
    index = index + jnp.where(odd, moved, 0)

    parts = block_count * SPLIT
    depth = rows_dev // parts
    later = lax.optimization_barrier(probes)
    pieces = [(later if i else probes)[i * depth : (i + 1) * depth] for i in range(parts)]
    peer = [across(pieces[i], "rows", 0) for i in range(parts)]
    far = [relayed(peer[i], "rows") for i in range(parts)]

    early = (block_count - 1) * SPLIT
    spots = [*range(block_count - 1), *range(block_count, 3 * block_count)]
    (left,) = near_step(near_blocks, samples, far[:early] + [probes] + peer, spots, index, near_count, flag, 0)
    spots = [block_count - 1]
    far_samples, partial = near_step(near_blocks, left, far[early:], spots, index, near_count, flag, 1, sketch)
    if halves == 2:
        other = across(partial, "samp", 0)
    else:
        partial, other = lax.psum(partial, "samp"), None
    leaf_sketch, gram, part, keep, send = leaf_products(flag, partial, other, far_samples)

    sums = []
    for h in range(LEVELS):
        part = part + across(part, "rows", h)
        sums.append(part)
    sums = jnp.stack(sums)
    sums_other = across(sums, "samp", 0) if halves == 2 else sums
    leaf_inverse, *inverses = factor_inverse(flag, gram, sums, sums_other)
    leaf_basis = lax.dot_general(leaf_sketch, leaf_inverse, (NT, ((), ())), precision=HIGH)

    value = keep + across(send, "rows", 0)
    values = [value]
    for h in range(1, LEVELS):
        value = value + across(value, "rows", h)
        values.append(value)
    lower = jnp.stack(values[:-1])
    lower_other = across(lower, "rows", 0)
    last_other = across(value, "rows", 0)
    reduced = reduce_early(flag, inverses[:-1], lower, lower_other)
    reduced = reduce_last(flag, inverses[-1], value, last_other, reduced)
    return (leaf_basis, reduced)


def solution(mesh):
    return jax.shard_map(
        leaf_and_levels,
        mesh=mesh,
        in_specs=(
            P("rows", "samp"),
            P("rows", "samp"),
            P("rows", None, None, None),
            P("rows", None),
            P("rows"),
            P("samp", None),
        ),
        out_specs=(P("rows", None), P(None, "rows", None, "samp")),
        check_vma=False,
    )
```

```python
import functools

import jax
import jax.numpy as jnp
from jax import lax
from jax.experimental import pallas as pl
from jax.experimental.pallas import tpu as pltpu
from jax.sharding import PartitionSpec as P

LEVELS = 4
LANES = 128
BASE = 64
WIDE = 16
SPLIT = 2
GRANT = 24 * 2**20
NN = ((1,), (0,))
NT = ((1,), (1,))
HIGH = lax.Precision.HIGH


def split(value):
    high = value.astype(jnp.bfloat16)
    return high, (value - high.astype(jnp.float32)).astype(jnp.bfloat16)


def dot3(left, right, dims):
    lh, ll = split(left)
    rh, rl = split(right)

    def product(a, b):
        return lax.dot_general(a, b, (dims, ((), ())), preferred_element_type=jnp.float32)

    return product(lh, rh) + (product(lh, rl) + product(ll, rh))


def pad_rows(block, start, total):
    parts = []
    if start:
        parts.append(jnp.zeros((start, block.shape[1]), block.dtype))
    parts.append(block)
    rest = total - start - block.shape[0]
    if rest:
        parts.append(jnp.zeros((rest, block.shape[1]), block.dtype))
    return jnp.concatenate(parts, axis=0) if len(parts) > 1 else block


def leaf_factor(work, out, start, base):
    fit = LANES // base
    tile = start // LANES * LANES
    off = start - tile
    lane = lax.broadcasted_iota(jnp.int32, (base, LANES), 1)
    row = lax.broadcasted_iota(jnp.int32, (base, LANES), 0)
    col = lane % base
    seg = lane // base
    groups = [range(g, min(g + fit, len(work))) for g in range(0, len(work), fit)]
    packs, pivots = [], []
    for group in groups:
        packed = jnp.where(col == row, 1.0, 0.0)
        for k in group:
            block = work[k][start:start + base, tile:tile + LANES]
            shift = (base * (k % fit) - off) % LANES
            if shift:
                block = pltpu.roll(block, shift, 1)
            packed = jnp.where(seg == k % fit, block, packed)
        packs.append(packed)
        pivots.append(jnp.ones((base, LANES), jnp.float32))
    for first in range(0, base, WIDE):
        low = first // 8 * 8
        rows = row[low:]
        cols = col[low:]
        for g in range(len(groups)):
            active = packs[g][low:]
            columns = [jnp.take_along_axis(active, (seg * base + first + t)[low:], axis=1) for t in range(WIDE)]
            for t in range(WIDE):
                j = first + t
                at = j - low
                pivot = columns[t][at:at + 1, :]
                pivots[g] = jnp.where(row == j, pivot, pivots[g])
                if j == base - 1:
                    break
                mult = jnp.where(rows > j, columns[t] * (1.0 / pivot), 0.0)
                for s in range(t + 1, WIDE):
                    columns[s] = columns[s] - mult * columns[s][at:at + 1, :]
                pivot_row = jnp.where(col[:1] == j, 1.0, active[at:at + 1, :])
                kept = jnp.where((rows > j) & (cols == j), 0.0, active)
                active = kept - mult * pivot_row
            packs[g] = active if low == 0 else jnp.concatenate([packs[g][:low], active], axis=0)
    inside = (lane >= off) & (lane < off + base)
    for g, group in enumerate(groups):
        unit = jnp.where(col < row, packs[g], jnp.where(col == row, 1.0, 0.0))
        unit = unit * lax.rsqrt(pivots[g])
        for k in group:
            shift = (off - base * (k % fit)) % LANES
            block = pltpu.roll(unit, shift, 1) if shift else unit
            out[k][start:start + base, tile:tile + LANES] = jnp.where(inside, block, 0.0)


def node_factor(work, out, start, size, base):
    if size == base:
        leaf_factor(work, out, start, base)
        return
    half = size // 2
    mid = start + half
    end = start + size
    node_factor(work, out, start, half, base)
    t1 = start // LANES * LANES
    t2 = mid // LANES * LANES
    width = max(LANES, half)
    kept = []
    for k in range(len(work)):
        x1 = out[k][start:mid, t1 : t1 + width]
        l21 = dot3(work[k][mid:end, t1 : t1 + width], x1, NT)
        work[k][mid:end, t2 : t2 + width] -= dot3(l21, pad_rows(l21, mid - t2, width), NT)
        kept.append(dot3(l21, x1, NN))
    node_factor(work, out, mid, half, base)
    for k in range(len(work)):
        x2 = out[k][mid:end, t2 : t2 + width]
        m21 = dot3(x2, pad_rows(kept[k], mid - t2, width), NN)
        out[k][mid:end, t1 : t1 + width] = x2 - m21 if t1 == t2 else -m21


def inverse_kernel(size, core_ref, gram_ref, mine_ref, other_ref, *refs):
    count = mine_ref.shape[0] + 1
    out, work = refs[:count], refs[count:]
    width = mine_ref.shape[2]
    swap = core_ref[0] == 1
    for k in range(count):
        if k == 0:
            work[k][...] = gram_ref[...]
        elif width == size:
            work[k][...] = mine_ref[k - 1]
        else:
            mine, other = mine_ref[k - 1], other_ref[k - 1]
            work[k][:, :width] = jnp.where(swap, other, mine)
            work[k][:, width:] = jnp.where(swap, mine, other)
        for t in range(0, size, LANES):
            out[k][:, t : t + LANES] = jnp.zeros((size, LANES), jnp.float32)
    node_factor(work, out, 0, size, BASE)


def factor_inverse(core, gram, mine, other):
    count, size = mine.shape[0] + 1, gram.shape[0]
    vmem = pl.BlockSpec(memory_space=pltpu.VMEM)
    smem = pl.BlockSpec(memory_space=pltpu.SMEM)
    return pl.pallas_call(
        functools.partial(inverse_kernel, size),
        out_shape=[pltpu.VMEM((size, size), jnp.float32)] * count,
        in_specs=[smem, vmem, vmem, vmem],
        out_specs=[vmem] * count,
        scratch_shapes=[pltpu.VMEM((size, size), jnp.float32)] * count,
        cost_estimate=pl.CostEstimate(flops=15 * 10**9, bytes_accessed=8 * count * size**2, transcendentals=0),
        compiler_params=pltpu.CompilerParams(vmem_limit_bytes=GRANT),
        name="factor_inverse",
    )(core, gram, mine, other)


def near_kernel(groups, first_slot, spots, sketched, index_ref, count_ref, flag_ref, blocks_ref, base_ref, *refs):
    pieces = refs[:groups]
    sketch_ref = refs[groups] if sketched else None
    rest = refs[groups + sketched :]
    out_ref, ext = rest[0], rest[-1]
    block_count, slot_count, size, _ = blocks_ref.shape
    at = 0
    for g in range(groups):
        depth = pieces[g].shape[0]
        ext[at : at + depth, :] = pieces[g][...]
        at += depth
    out_ref[...] = base_ref[...]
    for b in range(block_count):
        rows = pl.ds(b * size, size)
        for j in range(first_slot, slot_count):
            spot = index_ref[b, j]
            start = jnp.int32(0)
            here = jnp.bool_(False)
            for order, name in enumerate(spots):
                same = spot == name
                start = jnp.where(same, order * size, start)
                here = here | same

            @pl.when(here & (j < count_ref[b]))
            def _(b=b, j=j, rows=rows, start=start):
                piece = ext[pl.ds(pl.multiple_of(start, size), size), :]
                out_ref[rows, :] -= dot3(blocks_ref[b, j], piece, NN)

    if sketched:
        rest[1][...] = dot3(out_ref[...], sketch_ref[...], NN)


def near_step(blocks, base, pieces, spots, index, count, flag, first_slot, sketch=None):
    block_count, slot_count, size, _ = blocks.shape
    rows, width = base.shape
    total = sum(piece.shape[0] for piece in pieces)
    vmem = pl.BlockSpec(memory_space=pltpu.VMEM)
    smem = pl.BlockSpec(memory_space=pltpu.SMEM)
    extra = [] if sketch is None else [sketch]
    shapes = [(rows, width)] + [(rows, value.shape[1]) for value in extra]
    return pl.pallas_call(
        functools.partial(near_kernel, len(pieces), first_slot, tuple(spots), len(extra)),
        out_shape=[pltpu.VMEM(shape, jnp.float32) for shape in shapes],
        in_specs=[smem] * 3 + [vmem] * (2 + len(pieces) + len(extra)),
        out_specs=[vmem] * len(shapes),
        scratch_shapes=[pltpu.VMEM((total, width), jnp.float32)],
        cost_estimate=pl.CostEstimate(
            flops=6 * block_count * slot_count * size * size * width,
            bytes_accessed=4 * (total * width + 2 * rows * width + blocks.size),
            transcendentals=0,
        ),
        compiler_params=pltpu.CompilerParams(vmem_limit_bytes=GRANT),
        name="near_step",
    )(index, count, flag, blocks, base, *pieces, *extra)


def leaf_kernel(flag_ref, half_ref, other_ref, far_ref, sketch_ref, gram_ref, part_ref, keep_ref, send_ref, product):
    sketch = half_ref[...] + other_ref[...] if other_ref is not None else half_ref[...]
    sketch_ref[...] = sketch
    turned = sketch.T
    gram = dot3(turned, sketch, NN)
    gram_ref[...] = gram
    rank = gram.shape[0]
    width = part_ref.shape[1]
    part_ref[...] = jnp.where(flag_ref[0] == 1, gram[:, rank - width :], gram[:, :width])
    product[...] = dot3(turned, far_ref[...], NN)
    depth = keep_ref.shape[0]
    keep_ref[...] = product[pl.ds(pl.multiple_of(flag_ref[1], depth), depth), :]
    send_ref[...] = product[pl.ds(pl.multiple_of(flag_ref[2], depth), depth), :]


def leaf_products(flag, part, other, far):
    rows, rank = part.shape
    width = far.shape[1]
    vmem = pl.BlockSpec(memory_space=pltpu.VMEM)
    smem = pl.BlockSpec(memory_space=pltpu.SMEM)
    half = rank // 2
    shapes = [(rows, rank), (rank, rank), (rank, rank if other is None else half), (half, width), (half, width)]
    kernel = leaf_kernel
    args = [flag, part, other, far]
    if other is None:
        args = [flag, part, far]

        def kernel(flag_ref, part_ref, far_ref, *refs):
            leaf_kernel(flag_ref, part_ref, None, far_ref, *refs)

    return pl.pallas_call(
        kernel,
        out_shape=[pltpu.VMEM(shape, jnp.float32) for shape in shapes],
        in_specs=[smem] + [vmem] * (len(args) - 1),
        out_specs=[vmem] * len(shapes),
        scratch_shapes=[pltpu.VMEM((rank, width), jnp.float32)],
        cost_estimate=pl.CostEstimate(
            flops=6 * rows * rank * (rank + width), bytes_accessed=4 * rows * (3 * rank + width), transcendentals=0
        ),
        compiler_params=pltpu.CompilerParams(vmem_limit_bytes=GRANT),
        name="leaf_products",
    )(*args)


def staged(stage, flag_ref, mine, other):
    depth = mine.shape[0]
    stage[pl.ds(pl.multiple_of(flag_ref[1], depth), depth), :] = mine
    stage[pl.ds(pl.multiple_of(flag_ref[2], depth), depth), :] = other
    return stage[...]


def early_kernel(flag_ref, *refs):
    count = LEVELS - 1
    inverses, mine_ref, other_ref = refs[:count], refs[count], refs[count + 1]
    out_ref, stage, result, sems = refs[count + 2 :]
    copies = []
    for h in range(count):
        result[h] = dot3(inverses[h][...], staged(stage.at[h], flag_ref, mine_ref[h], other_ref[h]), NN)
        copies.append(pltpu.make_async_copy(result.at[h], out_ref.at[h, 0], sems.at[h]))
        copies[-1].start()
    for copy in copies:
        copy.wait()


def reduce_early(flag, inverses, mine, other):
    rank, width = inverses[0].shape[0], mine.shape[2]
    vmem = pl.BlockSpec(memory_space=pltpu.VMEM)
    smem = pl.BlockSpec(memory_space=pltpu.SMEM)
    count = LEVELS - 1
    return pl.pallas_call(
        early_kernel,
        out_shape=jax.ShapeDtypeStruct((LEVELS, 1, rank, width), jnp.float32),
        in_specs=[smem] + [vmem] * (count + 2),
        out_specs=pl.BlockSpec(memory_space=pl.ANY),
        scratch_shapes=[
            pltpu.VMEM((count, rank, width), jnp.float32),
            pltpu.VMEM((count, rank, width), jnp.float32),
            pltpu.SemaphoreType.DMA((count,)),
        ],
        cost_estimate=pl.CostEstimate(
            flops=6 * count * rank * rank * width, bytes_accessed=8 * count * rank * (rank + width), transcendentals=0
        ),
        compiler_params=pltpu.CompilerParams(vmem_limit_bytes=GRANT),
        name="reduce_early",
    )(flag, *inverses, mine, other)


def last_kernel(flag_ref, inverse_ref, mine_ref, other_ref, kept_ref, out_ref, stage, result, sem):
    result[...] = dot3(inverse_ref[...], staged(stage, flag_ref, mine_ref[...], other_ref[...]), NN)
    copy = pltpu.make_async_copy(result, out_ref.at[LEVELS - 1, 0], sem)
    copy.start()
    copy.wait()


def reduce_last(flag, inverse, mine, other, reduced):
    rank, width = inverse.shape[0], mine.shape[1]
    vmem = pl.BlockSpec(memory_space=pltpu.VMEM)
    smem = pl.BlockSpec(memory_space=pltpu.SMEM)
    hbm = pl.BlockSpec(memory_space=pl.ANY)
    return pl.pallas_call(
        last_kernel,
        out_shape=jax.ShapeDtypeStruct(reduced.shape, jnp.float32),
        in_specs=[smem] + [vmem] * 3 + [hbm],
        out_specs=hbm,
        scratch_shapes=[
            pltpu.VMEM((rank, width), jnp.float32),
            pltpu.VMEM((rank, width), jnp.float32),
            pltpu.SemaphoreType.DMA,
        ],
        input_output_aliases={4: 0},
        cost_estimate=pl.CostEstimate(
            flops=6 * rank * rank * width, bytes_accessed=8 * rank * (rank + width), transcendentals=0
        ),
        compiler_params=pltpu.CompilerParams(vmem_limit_bytes=GRANT),
        name="reduce_last",
    )(flag, inverse, mine, other, reduced)


def across(value, axis, bit):
    return lax.ppermute(value, axis, [(i, i ^ 1 << bit) for i in range(lax.axis_size(axis))])


def relayed(value, axis):
    count = lax.axis_size(axis)
    steps = [(i, i + 2 if i % 2 == 0 else i - 2) for i in range(count)]
    return lax.ppermute(value, axis, [(i, t) for i, t in steps if 0 <= t < count])


def leaf_and_levels(samples, probes, near_blocks, near_cols, near_count, sketch):
    rows_dev, _ = samples.shape
    block_size = near_blocks.shape[2]
    block_count = rows_dev // block_size
    rank = sketch.shape[1]
    position = lax.axis_index("rows")
    bits = [position >> h & 1 for h in range(LEVELS)]
    odd = bits[0] == 1
    halves = 2 if lax.axis_size("samp") == 2 else 1
    core = lax.axis_index("samp") % 2
    half = rank // 2
    flag = jnp.stack([core, bits[0] * half, half - bits[0] * half]).astype(jnp.int32)

    index = near_cols - (position * block_count - block_count)
    moved = jnp.where(index < block_count, 2 * block_count, jnp.where(index >= 2 * block_count, -2 * block_count, 0))
    index = index + jnp.where(odd, moved, 0)

    parts = block_count * SPLIT
    depth = rows_dev // parts
    later = lax.optimization_barrier(probes)
    pieces = [(later if i else probes)[i * depth : (i + 1) * depth] for i in range(parts)]
    peer = [across(pieces[i], "rows", 0) for i in range(parts)]
    far = [relayed(peer[i], "rows") for i in range(parts)]

    spots = [*range(block_count, 2 * block_count)]
    (left,) = near_step(near_blocks, samples, [probes], spots, index, near_count, near_count, 0)
    early = (block_count - 1) * SPLIT
    spots = [*range(block_count - 1), *range(2 * block_count, 3 * block_count)]
    (left,) = near_step(near_blocks, left, far[:early] + peer, spots, index, near_count, flag, 1)
    spots = [block_count - 1]
    far_samples, partial = near_step(near_blocks, left, far[early:], spots, index, near_count, flag, 1, sketch)
    if halves == 2:
        other = across(partial, "samp", 0)
    else:
        partial, other = lax.psum(partial, "samp"), None
    leaf_sketch, gram, part, keep, send = leaf_products(flag, partial, other, far_samples)

    sums = []
    for h in range(LEVELS):
        part = part + across(part, "rows", h)
        sums.append(part)
    sums = jnp.stack(sums)
    sums_other = across(sums, "samp", 0) if halves == 2 else sums
    leaf_inverse, *inverses = factor_inverse(flag, gram, sums, sums_other)
    leaf_basis = lax.dot_general(leaf_sketch, leaf_inverse, (NT, ((), ())), precision=HIGH)

    value = keep + across(send, "rows", 0)
    values = [value]
    for h in range(1, LEVELS):
        value = value + across(value, "rows", h)
        values.append(value)
    lower = jnp.stack(values[:-1])
    lower_other = across(lower, "rows", 0)
    last_other = across(value, "rows", 0)
    reduced = reduce_early(flag, inverses[:-1], lower, lower_other)
    reduced = reduce_last(flag, inverses[-1], value, last_other, reduced)
    return (leaf_basis, reduced)


def solution(mesh):
    return jax.shard_map(
        leaf_and_levels,
        mesh=mesh,
        in_specs=(
            P("rows", "samp"),
            P("rows", "samp"),
            P("rows", None, None, None),
            P("rows", None),
            P("rows"),
            P("samp", None),
        ),
        out_specs=(P("rows", None), P(None, "rows", None, "samp")),
        check_vma=False,
    )
```

```python
import functools

import jax
import jax.numpy as jnp
from jax import lax
from jax.experimental import pallas as pl
from jax.experimental.pallas import tpu as pltpu
from jax.sharding import PartitionSpec as P

LEVELS = 4
LANES = 128
BASE = 64
WIDE = 16
SPLIT = 2
GRANT = 16 * 2**20
NN = ((1,), (0,))
NT = ((1,), (1,))
HIGH = lax.Precision.HIGH


def split(value):
    high = value.astype(jnp.bfloat16)
    return high, (value - high.astype(jnp.float32)).astype(jnp.bfloat16)


def dot3(left, right, dims):
    lh, ll = split(left)
    rh, rl = split(right)

    def product(a, b):
        return lax.dot_general(a, b, (dims, ((), ())), preferred_element_type=jnp.float32)

    return product(lh, rh) + (product(lh, rl) + product(ll, rh))


def pad_rows(block, start, total):
    parts = []
    if start:
        parts.append(jnp.zeros((start, block.shape[1]), block.dtype))
    parts.append(block)
    rest = total - start - block.shape[0]
    if rest:
        parts.append(jnp.zeros((rest, block.shape[1]), block.dtype))
    return jnp.concatenate(parts, axis=0) if len(parts) > 1 else block


def leaf_factor(work, out, start, base):
    fit = LANES // base
    tile = start // LANES * LANES
    off = start - tile
    lane = lax.broadcasted_iota(jnp.int32, (base, LANES), 1)
    row = lax.broadcasted_iota(jnp.int32, (base, LANES), 0)
    col = lane % base
    seg = lane // base
    groups = [range(g, min(g + fit, len(work))) for g in range(0, len(work), fit)]
    packs, pivots = [], []
    for group in groups:
        packed = jnp.where(col == row, 1.0, 0.0)
        for k in group:
            block = work[k][start:start + base, tile:tile + LANES]
            shift = (base * (k % fit) - off) % LANES
            if shift:
                block = pltpu.roll(block, shift, 1)
            packed = jnp.where(seg == k % fit, block, packed)
        packs.append(packed)
        pivots.append(jnp.ones((base, LANES), jnp.float32))
    for first in range(0, base, WIDE):
        low = first // 8 * 8
        rows = row[low:]
        cols = col[low:]
        for g in range(len(groups)):
            active = packs[g][low:]
            columns = [jnp.take_along_axis(active, (seg * base + first + t)[low:], axis=1) for t in range(WIDE)]
            for t in range(WIDE):
                j = first + t
                at = j - low
                pivot = columns[t][at:at + 1, :]
                pivots[g] = jnp.where(row == j, pivot, pivots[g])
                if j == base - 1:
                    break
                mult = jnp.where(rows > j, columns[t] * (1.0 / pivot), 0.0)
                for s in range(t + 1, WIDE):
                    columns[s] = columns[s] - mult * columns[s][at:at + 1, :]
                pivot_row = jnp.where(col[:1] == j, 1.0, active[at:at + 1, :])
                kept = jnp.where((rows > j) & (cols == j), 0.0, active)
                active = kept - mult * pivot_row
            packs[g] = active if low == 0 else jnp.concatenate([packs[g][:low], active], axis=0)
    inside = (lane >= off) & (lane < off + base)
    for g, group in enumerate(groups):
        unit = jnp.where(col < row, packs[g], jnp.where(col == row, 1.0, 0.0))
        unit = unit * lax.rsqrt(pivots[g])
        for k in group:
            shift = (off - base * (k % fit)) % LANES
            block = pltpu.roll(unit, shift, 1) if shift else unit
            out[k][start:start + base, tile:tile + LANES] = jnp.where(inside, block, 0.0)


def node_factor(work, out, start, size, base):
    if size == base:
        leaf_factor(work, out, start, base)
        return
    half = size // 2
    mid = start + half
    end = start + size
    node_factor(work, out, start, half, base)
    t1 = start // LANES * LANES
    t2 = mid // LANES * LANES
    width = max(LANES, half)
    kept = []
    for k in range(len(work)):
        x1 = out[k][start:mid, t1 : t1 + width]
        l21 = dot3(work[k][mid:end, t1 : t1 + width], x1, NT)
        work[k][mid:end, t2 : t2 + width] -= dot3(l21, pad_rows(l21, mid - t2, width), NT)
        kept.append(dot3(l21, x1, NN))
    node_factor(work, out, mid, half, base)
    for k in range(len(work)):
        x2 = out[k][mid:end, t2 : t2 + width]
        m21 = dot3(x2, pad_rows(kept[k], mid - t2, width), NN)
        out[k][mid:end, t1 : t1 + width] = x2 - m21 if t1 == t2 else -m21


def inverse_kernel(size, core_ref, gram_ref, mine_ref, other_ref, *refs):
    count = mine_ref.shape[0] + 1
    out, work = refs[:count], refs[count:]
    width = mine_ref.shape[2]
    swap = core_ref[0] == 1
    for k in range(count):
        if k == 0:
            work[k][...] = gram_ref[...]
        elif width == size:
            work[k][...] = mine_ref[k - 1]
        else:
            mine, other = mine_ref[k - 1], other_ref[k - 1]
            work[k][:, :width] = jnp.where(swap, other, mine)
            work[k][:, width:] = jnp.where(swap, mine, other)
        for t in range(0, size, LANES):
            out[k][:, t : t + LANES] = jnp.zeros((size, LANES), jnp.float32)
    node_factor(work, out, 0, size, BASE)


def factor_inverse(core, gram, mine, other):
    count, size = mine.shape[0] + 1, gram.shape[0]
    vmem = pl.BlockSpec(memory_space=pltpu.VMEM)
    smem = pl.BlockSpec(memory_space=pltpu.SMEM)
    return pl.pallas_call(
        functools.partial(inverse_kernel, size),
        out_shape=[pltpu.VMEM((size, size), jnp.float32)] * count,
        in_specs=[smem, vmem, vmem, vmem],
        out_specs=[vmem] * count,
        scratch_shapes=[pltpu.VMEM((size, size), jnp.float32)] * count,
        cost_estimate=pl.CostEstimate(flops=15 * 10**9, bytes_accessed=8 * count * size**2, transcendentals=0),
        compiler_params=pltpu.CompilerParams(vmem_limit_bytes=GRANT),
        name="factor_inverse",
    )(core, gram, mine, other)


def near_kernel(groups, first_slot, spots, sketched, index_ref, count_ref, flag_ref, blocks_ref, base_ref, *refs):
    pieces = refs[:groups]
    sketch_ref = refs[groups] if sketched else None
    rest = refs[groups + sketched :]
    out_ref, ext = rest[0], rest[-1]
    block_count, slot_count, size, _ = blocks_ref.shape
    at = 0
    for g in range(groups):
        depth = pieces[g].shape[0]
        ext[at : at + depth, :] = pieces[g][...]
        at += depth
    out_ref[...] = base_ref[...]
    for b in range(block_count):
        rows = pl.ds(b * size, size)
        for j in range(first_slot, slot_count):
            spot = index_ref[b, j]
            start = jnp.int32(0)
            here = jnp.bool_(False)
            for order, name in enumerate(spots):
                same = spot == name
                start = jnp.where(same, order * size, start)
                here = here | same

            @pl.when(here & (j < count_ref[b]))
            def _(b=b, j=j, rows=rows, start=start):
                piece = ext[pl.ds(pl.multiple_of(start, size), size), :]
                out_ref[rows, :] -= dot3(blocks_ref[b, j], piece, NN)

    if sketched:
        rest[1][...] = dot3(out_ref[...], sketch_ref[...], NN)


def near_step(blocks, base, pieces, spots, index, count, flag, first_slot, sketch=None):
    block_count, slot_count, size, _ = blocks.shape
    rows, width = base.shape
    total = sum(piece.shape[0] for piece in pieces)
    vmem = pl.BlockSpec(memory_space=pltpu.VMEM)
    smem = pl.BlockSpec(memory_space=pltpu.SMEM)
    extra = [] if sketch is None else [sketch]
    shapes = [(rows, width)] + [(rows, value.shape[1]) for value in extra]
    return pl.pallas_call(
        functools.partial(near_kernel, len(pieces), first_slot, tuple(spots), len(extra)),
        out_shape=[pltpu.VMEM(shape, jnp.float32) for shape in shapes],
        in_specs=[smem] * 3 + [vmem] * (2 + len(pieces) + len(extra)),
        out_specs=[vmem] * len(shapes),
        scratch_shapes=[pltpu.VMEM((total, width), jnp.float32)],
        cost_estimate=pl.CostEstimate(
            flops=6 * block_count * slot_count * size * size * width,
            bytes_accessed=4 * (total * width + 2 * rows * width + blocks.size),
            transcendentals=0,
        ),
        compiler_params=pltpu.CompilerParams(vmem_limit_bytes=GRANT),
        name="near_step",
    )(index, count, flag, blocks, base, *pieces, *extra)


def leaf_kernel(flag_ref, half_ref, other_ref, far_ref, sketch_ref, gram_ref, part_ref, keep_ref, send_ref, product):
    sketch = half_ref[...] + other_ref[...] if other_ref is not None else half_ref[...]
    sketch_ref[...] = sketch
    turned = sketch.T
    gram = dot3(turned, sketch, NN)
    gram_ref[...] = gram
    rank = gram.shape[0]
    width = part_ref.shape[1]
    part_ref[...] = jnp.where(flag_ref[0] == 1, gram[:, rank - width :], gram[:, :width])
    product[...] = dot3(turned, far_ref[...], NN)
    depth = keep_ref.shape[0]
    keep_ref[...] = product[pl.ds(pl.multiple_of(flag_ref[1], depth), depth), :]
    send_ref[...] = product[pl.ds(pl.multiple_of(flag_ref[2], depth), depth), :]


def leaf_products(flag, part, other, far):
    rows, rank = part.shape
    width = far.shape[1]
    vmem = pl.BlockSpec(memory_space=pltpu.VMEM)
    smem = pl.BlockSpec(memory_space=pltpu.SMEM)
    half = rank // 2
    shapes = [(rows, rank), (rank, rank), (rank, rank if other is None else half), (half, width), (half, width)]
    kernel = leaf_kernel
    args = [flag, part, other, far]
    if other is None:
        args = [flag, part, far]

        def kernel(flag_ref, part_ref, far_ref, *refs):
            leaf_kernel(flag_ref, part_ref, None, far_ref, *refs)

    return pl.pallas_call(
        kernel,
        out_shape=[pltpu.VMEM(shape, jnp.float32) for shape in shapes],
        in_specs=[smem] + [vmem] * (len(args) - 1),
        out_specs=[vmem] * len(shapes),
        scratch_shapes=[pltpu.VMEM((rank, width), jnp.float32)],
        cost_estimate=pl.CostEstimate(
            flops=6 * rows * rank * (rank + width), bytes_accessed=4 * rows * (3 * rank + width), transcendentals=0
        ),
        compiler_params=pltpu.CompilerParams(vmem_limit_bytes=GRANT),
        name="leaf_products",
    )(*args)


def staged(stage, flag_ref, mine, other):
    depth = mine.shape[0]
    stage[pl.ds(pl.multiple_of(flag_ref[1], depth), depth), :] = mine
    stage[pl.ds(pl.multiple_of(flag_ref[2], depth), depth), :] = other
    return stage[...]


def early_kernel(flag_ref, *refs):
    count = LEVELS - 1
    inverses, mine_ref, other_ref = refs[:count], refs[count], refs[count + 1]
    out_ref, stage, result, sems = refs[count + 2 :]
    copies = []
    for h in range(count):
        result[h] = dot3(inverses[h][...], staged(stage.at[h], flag_ref, mine_ref[h], other_ref[h]), NN)
        copies.append(pltpu.make_async_copy(result.at[h], out_ref.at[h, 0], sems.at[h]))
        copies[-1].start()
    for copy in copies:
        copy.wait()


def reduce_early(flag, inverses, mine, other):
    rank, width = inverses[0].shape[0], mine.shape[2]
    vmem = pl.BlockSpec(memory_space=pltpu.VMEM)
    smem = pl.BlockSpec(memory_space=pltpu.SMEM)
    count = LEVELS - 1
    return pl.pallas_call(
        early_kernel,
        out_shape=jax.ShapeDtypeStruct((LEVELS, 1, rank, width), jnp.float32),
        in_specs=[smem] + [vmem] * (count + 2),
        out_specs=pl.BlockSpec(memory_space=pl.ANY),
        scratch_shapes=[
            pltpu.VMEM((count, rank, width), jnp.float32),
            pltpu.VMEM((count, rank, width), jnp.float32),
            pltpu.SemaphoreType.DMA((count,)),
        ],
        cost_estimate=pl.CostEstimate(
            flops=6 * count * rank * rank * width, bytes_accessed=8 * count * rank * (rank + width), transcendentals=0
        ),
        compiler_params=pltpu.CompilerParams(vmem_limit_bytes=GRANT),
        name="reduce_early",
    )(flag, *inverses, mine, other)


def last_kernel(flag_ref, inverse_ref, mine_ref, other_ref, kept_ref, out_ref, stage, result, sem):
    result[...] = dot3(inverse_ref[...], staged(stage, flag_ref, mine_ref[...], other_ref[...]), NN)
    copy = pltpu.make_async_copy(result, out_ref.at[LEVELS - 1, 0], sem)
    copy.start()
    copy.wait()


def reduce_last(flag, inverse, mine, other, reduced):
    rank, width = inverse.shape[0], mine.shape[1]
    vmem = pl.BlockSpec(memory_space=pltpu.VMEM)
    smem = pl.BlockSpec(memory_space=pltpu.SMEM)
    hbm = pl.BlockSpec(memory_space=pl.ANY)
    return pl.pallas_call(
        last_kernel,
        out_shape=jax.ShapeDtypeStruct(reduced.shape, jnp.float32),
        in_specs=[smem] + [vmem] * 3 + [hbm],
        out_specs=hbm,
        scratch_shapes=[
            pltpu.VMEM((rank, width), jnp.float32),
            pltpu.VMEM((rank, width), jnp.float32),
            pltpu.SemaphoreType.DMA,
        ],
        input_output_aliases={4: 0},
        cost_estimate=pl.CostEstimate(
            flops=6 * rank * rank * width, bytes_accessed=8 * rank * (rank + width), transcendentals=0
        ),
        compiler_params=pltpu.CompilerParams(vmem_limit_bytes=GRANT),
        name="reduce_last",
    )(flag, inverse, mine, other, reduced)


def across(value, axis, bit):
    return lax.ppermute(value, axis, [(i, i ^ 1 << bit) for i in range(lax.axis_size(axis))])


def relayed(value, axis):
    count = lax.axis_size(axis)
    steps = [(i, i + 2 if i % 2 == 0 else i - 2) for i in range(count)]
    return lax.ppermute(value, axis, [(i, t) for i, t in steps if 0 <= t < count])


def leaf_and_levels(samples, probes, near_blocks, near_cols, near_count, sketch):
    rows_dev, _ = samples.shape
    block_size = near_blocks.shape[2]
    block_count = rows_dev // block_size
    rank = sketch.shape[1]
    position = lax.axis_index("rows")
    bits = [position >> h & 1 for h in range(LEVELS)]
    odd = bits[0] == 1
    halves = 2 if lax.axis_size("samp") == 2 else 1
    core = lax.axis_index("samp") % 2
    half = rank // 2
    flag = jnp.stack([core, bits[0] * half, half - bits[0] * half]).astype(jnp.int32)

    index = near_cols - (position * block_count - block_count)
    moved = jnp.where(index < block_count, 2 * block_count, jnp.where(index >= 2 * block_count, -2 * block_count, 0))
    index = index + jnp.where(odd, moved, 0)

    parts = block_count * SPLIT
    depth = rows_dev // parts
    later = lax.optimization_barrier(probes)
    pieces = [(later if i else probes)[i * depth : (i + 1) * depth] for i in range(parts)]
    peer = [across(pieces[i], "rows", 0) for i in range(parts)]
    far = [relayed(peer[i], "rows") for i in range(parts)]

    early = (block_count - 1) * SPLIT
    spots = [*range(block_count - 1), *range(block_count, 3 * block_count)]
    (left,) = near_step(near_blocks, samples, far[:early] + [probes] + peer, spots, index, near_count, flag, 0)
    spots = [block_count - 1]
    far_samples, partial = near_step(near_blocks, left, far[early:], spots, index, near_count, flag, 1, sketch)
    if halves == 2:
        other = across(partial, "samp", 0)
    else:
        partial, other = lax.psum(partial, "samp"), None
    leaf_sketch, gram, part, keep, send = leaf_products(flag, partial, other, far_samples)

    sums = []
    for h in range(LEVELS):
        part = part + across(part, "rows", h)
        sums.append(part)
    sums = jnp.stack(sums)
    sums_other = across(sums, "samp", 0) if halves == 2 else sums
    leaf_inverse, *inverses = factor_inverse(flag, gram, sums, sums_other)
    leaf_basis = lax.dot_general(leaf_sketch, leaf_inverse, (NT, ((), ())), precision=HIGH)

    value = keep + across(send, "rows", 0)
    values = [value]
    for h in range(1, LEVELS):
        value = value + across(value, "rows", h)
        values.append(value)
    lower = jnp.stack(values[:-1])
    lower_other = across(lower, "rows", 0)
    last_other = across(value, "rows", 0)
    reduced = reduce_early(flag, inverses[:-1], lower, lower_other)
    reduced = reduce_last(flag, inverses[-1], value, last_other, reduced)
    return (leaf_basis, reduced)


def solution(mesh):
    return jax.shard_map(
        leaf_and_levels,
        mesh=mesh,
        in_specs=(
            P("rows", "samp"),
            P("rows", "samp"),
            P("rows", None, None, None),
            P("rows", None),
            P("rows"),
            P("samp", None),
        ),
        out_specs=(P("rows", None), P(None, "rows", None, "samp")),
        check_vma=False,
    )
```

```python
import functools

import jax
import jax.numpy as jnp
from jax import lax
from jax.experimental import pallas as pl
from jax.experimental.pallas import tpu as pltpu
from jax.sharding import PartitionSpec as P

LEVELS = 4
LANES = 128
BASE = 64
WIDE = 16
SPLIT = 2
GRANT = 16 * 2**20
NN = ((1,), (0,))
NT = ((1,), (1,))
HIGH = lax.Precision.HIGH


def split(value):
    high = value.astype(jnp.bfloat16)
    return high, (value - high.astype(jnp.float32)).astype(jnp.bfloat16)


def dot3(left, right, dims):
    lh, ll = split(left)
    rh, rl = split(right)

    def product(a, b):
        return lax.dot_general(a, b, (dims, ((), ())), preferred_element_type=jnp.float32)

    return product(lh, rh) + (product(lh, rl) + product(ll, rh))


def pad_rows(block, start, total):
    parts = []
    if start:
        parts.append(jnp.zeros((start, block.shape[1]), block.dtype))
    parts.append(block)
    rest = total - start - block.shape[0]
    if rest:
        parts.append(jnp.zeros((rest, block.shape[1]), block.dtype))
    return jnp.concatenate(parts, axis=0) if len(parts) > 1 else block


def leaf_factor(work, out, start, base):
    fit = LANES // base
    tile = start // LANES * LANES
    off = start - tile
    lane = lax.broadcasted_iota(jnp.int32, (base, LANES), 1)
    row = lax.broadcasted_iota(jnp.int32, (base, LANES), 0)
    col = lane % base
    seg = lane // base
    groups = [range(g, min(g + fit, len(work))) for g in range(0, len(work), fit)]
    packs, pivots = [], []
    for group in groups:
        packed = jnp.where(col == row, 1.0, 0.0)
        for k in group:
            block = work[k][start:start + base, tile:tile + LANES]
            shift = (base * (k % fit) - off) % LANES
            if shift:
                block = pltpu.roll(block, shift, 1)
            packed = jnp.where(seg == k % fit, block, packed)
        packs.append(packed)
        pivots.append(jnp.ones((base, LANES), jnp.float32))
    for first in range(0, base, WIDE):
        low = first // 8 * 8
        rows = row[low:]
        cols = col[low:]
        for g in range(len(groups)):
            active = packs[g][low:]
            columns = [jnp.take_along_axis(active, (seg * base + first + t)[low:], axis=1) for t in range(WIDE)]
            for t in range(WIDE):
                j = first + t
                at = j - low
                pivot = columns[t][at:at + 1, :]
                pivots[g] = jnp.where(row == j, pivot, pivots[g])
                if j == base - 1:
                    break
                mult = jnp.where(rows > j, columns[t] * (1.0 / pivot), 0.0)
                for s in range(t + 1, WIDE):
                    columns[s] = columns[s] - mult * columns[s][at:at + 1, :]
                pivot_row = jnp.where(col[:1] == j, 1.0, active[at:at + 1, :])
                kept = jnp.where((rows > j) & (cols == j), 0.0, active)
                active = kept - mult * pivot_row
            packs[g] = active if low == 0 else jnp.concatenate([packs[g][:low], active], axis=0)
    inside = (lane >= off) & (lane < off + base)
    for g, group in enumerate(groups):
        unit = jnp.where(col < row, packs[g], jnp.where(col == row, 1.0, 0.0))
        unit = unit * lax.rsqrt(pivots[g])
        for k in group:
            shift = (off - base * (k % fit)) % LANES
            block = pltpu.roll(unit, shift, 1) if shift else unit
            out[k][start:start + base, tile:tile + LANES] = jnp.where(inside, block, 0.0)


def node_factor(work, out, start, size, base):
    if size == base:
        leaf_factor(work, out, start, base)
        return
    half = size // 2
    mid = start + half
    end = start + size
    node_factor(work, out, start, half, base)
    t1 = start // LANES * LANES
    t2 = mid // LANES * LANES
    width = max(LANES, half)
    kept = []
    for k in range(len(work)):
        x1 = out[k][start:mid, t1 : t1 + width]
        l21 = dot3(work[k][mid:end, t1 : t1 + width], x1, NT)
        work[k][mid:end, t2 : t2 + width] -= dot3(l21, pad_rows(l21, mid - t2, width), NT)
        kept.append(dot3(l21, x1, NN))
    node_factor(work, out, mid, half, base)
    for k in range(len(work)):
        x2 = out[k][mid:end, t2 : t2 + width]
        m21 = dot3(x2, pad_rows(kept[k], mid - t2, width), NN)
        out[k][mid:end, t1 : t1 + width] = x2 - m21 if t1 == t2 else -m21


def inverse_kernel(size, core_ref, gram_ref, mine_ref, other_ref, *refs):
    count = mine_ref.shape[0] + 1
    out, work = refs[:count], refs[count:]
    width = mine_ref.shape[2]
    swap = core_ref[0] == 1
    for k in range(count):
        if k == 0:
            work[k][...] = gram_ref[...]
        elif width == size:
            work[k][...] = mine_ref[k - 1]
        else:
            mine, other = mine_ref[k - 1], other_ref[k - 1]
            work[k][:, :width] = jnp.where(swap, other, mine)
            work[k][:, width:] = jnp.where(swap, mine, other)
        for t in range(0, size, LANES):
            out[k][:, t : t + LANES] = jnp.zeros((size, LANES), jnp.float32)
    node_factor(work, out, 0, size, BASE)


def factor_inverse(core, gram, mine, other):
    count, size = mine.shape[0] + 1, gram.shape[0]
    vmem = pl.BlockSpec(memory_space=pltpu.VMEM)
    smem = pl.BlockSpec(memory_space=pltpu.SMEM)
    return pl.pallas_call(
        functools.partial(inverse_kernel, size),
        out_shape=[pltpu.VMEM((size, size), jnp.float32)] * count,
        in_specs=[smem, vmem, vmem, vmem],
        out_specs=[vmem] * count,
        scratch_shapes=[pltpu.VMEM((size, size), jnp.float32)] * count,
        cost_estimate=pl.CostEstimate(flops=15 * 10**9, bytes_accessed=8 * count * size**2, transcendentals=0),
        compiler_params=pltpu.CompilerParams(vmem_limit_bytes=GRANT),
        name="factor_inverse",
    )(core, gram, mine, other)


def near_kernel(groups, first_slot, spots, sketched, loads, index_ref, count_ref, flag_ref, blocks_ref, base_ref, *refs):
    pieces = refs[:groups]
    sketch_ref = refs[groups] if sketched else None
    rest = refs[groups + sketched :]
    out_ref, ext = rest[0], rest[-2] if loads else rest[-1]
    block_count, slot_count, size, _ = blocks_ref.shape
    held = rest[1] if loads else blocks_ref
    copies = {}
    if loads:
        for j in range(slot_count):
            for b in range(block_count):
                copies[b, j] = pltpu.make_async_copy(blocks_ref.at[b, j], held.at[b, j], rest[-1].at[b, j])
                copies[b, j].start()
    at = 0
    for g in range(groups):
        depth = pieces[g].shape[0]
        ext[at : at + depth, :] = pieces[g][...]
        at += depth
    out_ref[...] = base_ref[...]
    for j in range(first_slot, slot_count):
        for b in range(block_count):
            rows = pl.ds(b * size, size)
            if loads:
                copies[b, j].wait()
            spot = index_ref[b, j]
            start = jnp.int32(0)
            here = jnp.bool_(False)
            for order, name in enumerate(spots):
                same = spot == name
                start = jnp.where(same, order * size, start)
                here = here | same

            @pl.when(here & (j < count_ref[b]))
            def _(b=b, j=j, rows=rows, start=start):
                piece = ext[pl.ds(pl.multiple_of(start, size), size), :]
                out_ref[rows, :] -= dot3(held[b, j], piece, NN)

    if sketched:
        rest[1][...] = dot3(out_ref[...], sketch_ref[...], NN)


def near_step(blocks, base, pieces, spots, index, count, flag, first_slot, sketch=None, loads=False):
    block_count, slot_count, size, _ = blocks.shape
    rows, width = base.shape
    total = sum(piece.shape[0] for piece in pieces)
    vmem = pl.BlockSpec(memory_space=pltpu.VMEM)
    smem = pl.BlockSpec(memory_space=pltpu.SMEM)
    extra = [] if sketch is None else [sketch]
    shapes = [(rows, width)] + [(rows, value.shape[1]) for value in extra] + [blocks.shape] * loads
    source = pl.BlockSpec(memory_space=pltpu.HBM) if loads else vmem
    scratch = [pltpu.VMEM((total, width), jnp.float32)]
    if loads:
        scratch.append(pltpu.SemaphoreType.DMA((block_count, slot_count)))
    return pl.pallas_call(
        functools.partial(near_kernel, len(pieces), first_slot, tuple(spots), len(extra), loads),
        out_shape=[pltpu.VMEM(shape, jnp.float32) for shape in shapes],
        in_specs=[smem] * 3 + [source] + [vmem] * (1 + len(pieces) + len(extra)),
        out_specs=[vmem] * len(shapes),
        scratch_shapes=scratch,
        cost_estimate=pl.CostEstimate(
            flops=6 * block_count * slot_count * size * size * width,
            bytes_accessed=4 * (total * width + 2 * rows * width + blocks.size),
            transcendentals=0,
        ),
        compiler_params=pltpu.CompilerParams(vmem_limit_bytes=GRANT),
        name="near_step",
    )(index, count, flag, blocks, base, *pieces, *extra)


def leaf_kernel(flag_ref, half_ref, other_ref, far_ref, sketch_ref, gram_ref, part_ref, keep_ref, send_ref, product):
    sketch = half_ref[...] + other_ref[...] if other_ref is not None else half_ref[...]
    sketch_ref[...] = sketch
    turned = sketch.T
    gram = dot3(turned, sketch, NN)
    gram_ref[...] = gram
    rank = gram.shape[0]
    width = part_ref.shape[1]
    part_ref[...] = jnp.where(flag_ref[0] == 1, gram[:, rank - width :], gram[:, :width])
    product[...] = dot3(turned, far_ref[...], NN)
    depth = keep_ref.shape[0]
    keep_ref[...] = product[pl.ds(pl.multiple_of(flag_ref[1], depth), depth), :]
    send_ref[...] = product[pl.ds(pl.multiple_of(flag_ref[2], depth), depth), :]


def leaf_products(flag, part, other, far):
    rows, rank = part.shape
    width = far.shape[1]
    vmem = pl.BlockSpec(memory_space=pltpu.VMEM)
    smem = pl.BlockSpec(memory_space=pltpu.SMEM)
    half = rank // 2
    shapes = [(rows, rank), (rank, rank), (rank, rank if other is None else half), (half, width), (half, width)]
    kernel = leaf_kernel
    args = [flag, part, other, far]
    if other is None:
        args = [flag, part, far]

        def kernel(flag_ref, part_ref, far_ref, *refs):
            leaf_kernel(flag_ref, part_ref, None, far_ref, *refs)

    return pl.pallas_call(
        kernel,
        out_shape=[pltpu.VMEM(shape, jnp.float32) for shape in shapes],
        in_specs=[smem] + [vmem] * (len(args) - 1),
        out_specs=[vmem] * len(shapes),
        scratch_shapes=[pltpu.VMEM((rank, width), jnp.float32)],
        cost_estimate=pl.CostEstimate(
            flops=6 * rows * rank * (rank + width), bytes_accessed=4 * rows * (3 * rank + width), transcendentals=0
        ),
        compiler_params=pltpu.CompilerParams(vmem_limit_bytes=GRANT),
        name="leaf_products",
    )(*args)


def staged(stage, flag_ref, mine, other):
    depth = mine.shape[0]
    stage[pl.ds(pl.multiple_of(flag_ref[1], depth), depth), :] = mine
    stage[pl.ds(pl.multiple_of(flag_ref[2], depth), depth), :] = other
    return stage[...]


def early_kernel(flag_ref, *refs):
    count = LEVELS - 1
    inverses, mine_ref, other_ref = refs[:count], refs[count], refs[count + 1]
    out_ref, stage, result, sems = refs[count + 2 :]
    copies = []
    for h in range(count):
        result[h] = dot3(inverses[h][...], staged(stage.at[h], flag_ref, mine_ref[h], other_ref[h]), NN)
        copies.append(pltpu.make_async_copy(result.at[h], out_ref.at[h, 0], sems.at[h]))
        copies[-1].start()
    for copy in copies:
        copy.wait()


def reduce_early(flag, inverses, mine, other):
    rank, width = inverses[0].shape[0], mine.shape[2]
    vmem = pl.BlockSpec(memory_space=pltpu.VMEM)
    smem = pl.BlockSpec(memory_space=pltpu.SMEM)
    count = LEVELS - 1
    return pl.pallas_call(
        early_kernel,
        out_shape=jax.ShapeDtypeStruct((LEVELS, 1, rank, width), jnp.float32),
        in_specs=[smem] + [vmem] * (count + 2),
        out_specs=pl.BlockSpec(memory_space=pl.ANY),
        scratch_shapes=[
            pltpu.VMEM((count, rank, width), jnp.float32),
            pltpu.VMEM((count, rank, width), jnp.float32),
            pltpu.SemaphoreType.DMA((count,)),
        ],
        cost_estimate=pl.CostEstimate(
            flops=6 * count * rank * rank * width, bytes_accessed=8 * count * rank * (rank + width), transcendentals=0
        ),
        compiler_params=pltpu.CompilerParams(vmem_limit_bytes=GRANT),
        name="reduce_early",
    )(flag, *inverses, mine, other)


def last_kernel(flag_ref, inverse_ref, mine_ref, other_ref, kept_ref, out_ref, stage, result, sem):
    result[...] = dot3(inverse_ref[...], staged(stage, flag_ref, mine_ref[...], other_ref[...]), NN)
    copy = pltpu.make_async_copy(result, out_ref.at[LEVELS - 1, 0], sem)
    copy.start()
    copy.wait()


def reduce_last(flag, inverse, mine, other, reduced):
    rank, width = inverse.shape[0], mine.shape[1]
    vmem = pl.BlockSpec(memory_space=pltpu.VMEM)
    smem = pl.BlockSpec(memory_space=pltpu.SMEM)
    hbm = pl.BlockSpec(memory_space=pl.ANY)
    return pl.pallas_call(
        last_kernel,
        out_shape=jax.ShapeDtypeStruct(reduced.shape, jnp.float32),
        in_specs=[smem] + [vmem] * 3 + [hbm],
        out_specs=hbm,
        scratch_shapes=[
            pltpu.VMEM((rank, width), jnp.float32),
            pltpu.VMEM((rank, width), jnp.float32),
            pltpu.SemaphoreType.DMA,
        ],
        input_output_aliases={4: 0},
        cost_estimate=pl.CostEstimate(
            flops=6 * rank * rank * width, bytes_accessed=8 * rank * (rank + width), transcendentals=0
        ),
        compiler_params=pltpu.CompilerParams(vmem_limit_bytes=GRANT),
        name="reduce_last",
    )(flag, inverse, mine, other, reduced)


def across(value, axis, bit):
    return lax.ppermute(value, axis, [(i, i ^ 1 << bit) for i in range(lax.axis_size(axis))])


def relayed(value, axis):
    count = lax.axis_size(axis)
    steps = [(i, i + 2 if i % 2 == 0 else i - 2) for i in range(count)]
    return lax.ppermute(value, axis, [(i, t) for i, t in steps if 0 <= t < count])


def leaf_and_levels(samples, probes, near_blocks, near_cols, near_count, sketch):
    rows_dev, _ = samples.shape
    block_size = near_blocks.shape[2]
    block_count = rows_dev // block_size
    rank = sketch.shape[1]
    position = lax.axis_index("rows")
    bits = [position >> h & 1 for h in range(LEVELS)]
    odd = bits[0] == 1
    halves = 2 if lax.axis_size("samp") == 2 else 1
    core = lax.axis_index("samp") % 2
    half = rank // 2
    flag = jnp.stack([core, bits[0] * half, half - bits[0] * half]).astype(jnp.int32)

    index = near_cols - (position * block_count - block_count)
    moved = jnp.where(index < block_count, 2 * block_count, jnp.where(index >= 2 * block_count, -2 * block_count, 0))
    index = index + jnp.where(odd, moved, 0)

    parts = block_count * SPLIT
    depth = rows_dev // parts
    later = lax.optimization_barrier(probes)
    pieces = [(later if i else probes)[i * depth : (i + 1) * depth] for i in range(parts)]
    peer = [across(pieces[i], "rows", 0) for i in range(parts)]
    far = [relayed(peer[i], "rows") for i in range(parts)]

    early = (block_count - 1) * SPLIT
    spots = [*range(block_count - 1), *range(block_count, 3 * block_count)]
    pieces = far[:early] + [probes] + peer
    stored = pltpu.with_memory_space_constraint(near_blocks, pltpu.HBM)
    left, held = near_step(stored, samples, pieces, spots, index, near_count, flag, 0, loads=True)
    spots = [block_count - 1]
    far_samples, partial = near_step(held, left, far[early:], spots, index, near_count, flag, 1, sketch)
    if halves == 2:
        other = across(partial, "samp", 0)
    else:
        partial, other = lax.psum(partial, "samp"), None
    leaf_sketch, gram, part, keep, send = leaf_products(flag, partial, other, far_samples)

    sums = []
    for h in range(LEVELS):
        part = part + across(part, "rows", h)
        sums.append(part)
    sums = jnp.stack(sums)
    sums_other = across(sums, "samp", 0) if halves == 2 else sums
    leaf_inverse, *inverses = factor_inverse(flag, gram, sums, sums_other)
    leaf_basis = lax.dot_general(leaf_sketch, leaf_inverse, (NT, ((), ())), precision=HIGH)

    value = keep + across(send, "rows", 0)
    values = [value]
    for h in range(1, LEVELS):
        value = value + across(value, "rows", h)
        values.append(value)
    lower = jnp.stack(values[:-1])
    lower_other = across(lower, "rows", 0)
    last_other = across(value, "rows", 0)
    reduced = reduce_early(flag, inverses[:-1], lower, lower_other)
    reduced = reduce_last(flag, inverses[-1], value, last_other, reduced)
    return (leaf_basis, reduced)


def solution(mesh):
    return jax.shard_map(
        leaf_and_levels,
        mesh=mesh,
        in_specs=(
            P("rows", "samp"),
            P("rows", "samp"),
            P("rows", None, None, None),
            P("rows", None),
            P("rows"),
            P("samp", None),
        ),
        out_specs=(P("rows", None), P(None, "rows", None, "samp")),
        check_vma=False,
    )
```

```python
import functools

import jax
import jax.numpy as jnp
from jax import lax
from jax.experimental import pallas as pl
from jax.experimental.pallas import tpu as pltpu
from jax.sharding import PartitionSpec as P

LEVELS = 4
LANES = 128
BASE = 64
WIDE = 16
SPLIT = 2
GRANT = 16 * 2**20
NN = ((1,), (0,))
NT = ((1,), (1,))
HIGH = lax.Precision.HIGH


def split(value):
    high = value.astype(jnp.bfloat16)
    return high, (value - high.astype(jnp.float32)).astype(jnp.bfloat16)


def dot3(left, right, dims):
    lh, ll = split(left)
    rh, rl = split(right)

    def product(a, b):
        return lax.dot_general(a, b, (dims, ((), ())), preferred_element_type=jnp.float32)

    return product(lh, rh) + (product(lh, rl) + product(ll, rh))


def pad_rows(block, start, total):
    parts = []
    if start:
        parts.append(jnp.zeros((start, block.shape[1]), block.dtype))
    parts.append(block)
    rest = total - start - block.shape[0]
    if rest:
        parts.append(jnp.zeros((rest, block.shape[1]), block.dtype))
    return jnp.concatenate(parts, axis=0) if len(parts) > 1 else block


def leaf_factor(work, out, start, base):
    fit = LANES // base
    tile = start // LANES * LANES
    off = start - tile
    lane = lax.broadcasted_iota(jnp.int32, (base, LANES), 1)
    row = lax.broadcasted_iota(jnp.int32, (base, LANES), 0)
    col = lane % base
    seg = lane // base
    groups = [range(g, min(g + fit, len(work))) for g in range(0, len(work), fit)]
    packs, pivots = [], []
    for group in groups:
        packed = jnp.where(col == row, 1.0, 0.0)
        for k in group:
            block = work[k][start:start + base, tile:tile + LANES]
            shift = (base * (k % fit) - off) % LANES
            if shift:
                block = pltpu.roll(block, shift, 1)
            packed = jnp.where(seg == k % fit, block, packed)
        packs.append(packed)
        pivots.append(jnp.ones((base, LANES), jnp.float32))
    for first in range(0, base, WIDE):
        low = first // 8 * 8
        rows = row[low:]
        cols = col[low:]
        for g in range(len(groups)):
            active = packs[g][low:]
            columns = [jnp.take_along_axis(active, (seg * base + first + t)[low:], axis=1) for t in range(WIDE)]
            for t in range(WIDE):
                j = first + t
                at = j - low
                pivot = columns[t][at:at + 1, :]
                pivots[g] = jnp.where(row == j, pivot, pivots[g])
                if j == base - 1:
                    break
                mult = jnp.where(rows > j, columns[t] * (1.0 / pivot), 0.0)
                for s in range(t + 1, WIDE):
                    columns[s] = columns[s] - mult * columns[s][at:at + 1, :]
                pivot_row = jnp.where(col[:1] == j, 1.0, active[at:at + 1, :])
                kept = jnp.where((rows > j) & (cols == j), 0.0, active)
                active = kept - mult * pivot_row
            packs[g] = active if low == 0 else jnp.concatenate([packs[g][:low], active], axis=0)
    inside = (lane >= off) & (lane < off + base)
    for g, group in enumerate(groups):
        unit = jnp.where(col < row, packs[g], jnp.where(col == row, 1.0, 0.0))
        unit = unit * lax.rsqrt(pivots[g])
        for k in group:
            shift = (off - base * (k % fit)) % LANES
            block = pltpu.roll(unit, shift, 1) if shift else unit
            out[k][start:start + base, tile:tile + LANES] = jnp.where(inside, block, 0.0)


def node_factor(work, out, start, size, base):
    if size == base:
        leaf_factor(work, out, start, base)
        return
    half = size // 2
    mid = start + half
    end = start + size
    node_factor(work, out, start, half, base)
    t1 = start // LANES * LANES
    t2 = mid // LANES * LANES
    width = max(LANES, half)
    kept = []
    for k in range(len(work)):
        x1 = out[k][start:mid, t1 : t1 + width]
        l21 = dot3(work[k][mid:end, t1 : t1 + width], x1, NT)
        work[k][mid:end, t2 : t2 + width] -= dot3(l21, pad_rows(l21, mid - t2, width), NT)
        kept.append(dot3(l21, x1, NN))
    node_factor(work, out, mid, half, base)
    for k in range(len(work)):
        x2 = out[k][mid:end, t2 : t2 + width]
        m21 = dot3(x2, pad_rows(kept[k], mid - t2, width), NN)
        out[k][mid:end, t1 : t1 + width] = x2 - m21 if t1 == t2 else -m21


def inverse_kernel(size, core_ref, gram_ref, mine_ref, other_ref, *refs):
    count = mine_ref.shape[0] + 1
    out, work = refs[:count], refs[count:]
    width = mine_ref.shape[2]
    swap = core_ref[0] == 1
    for k in range(count):
        if k == 0:
            work[k][...] = gram_ref[...]
        elif width == size:
            work[k][...] = mine_ref[k - 1]
        else:
            mine, other = mine_ref[k - 1], other_ref[k - 1]
            work[k][:, :width] = jnp.where(swap, other, mine)
            work[k][:, width:] = jnp.where(swap, mine, other)
        for t in range(0, size, LANES):
            out[k][:, t : t + LANES] = jnp.zeros((size, LANES), jnp.float32)
    node_factor(work, out, 0, size, BASE)


def factor_inverse(core, gram, mine, other):
    count, size = mine.shape[0] + 1, gram.shape[0]
    vmem = pl.BlockSpec(memory_space=pltpu.VMEM)
    smem = pl.BlockSpec(memory_space=pltpu.SMEM)
    return pl.pallas_call(
        functools.partial(inverse_kernel, size),
        out_shape=[pltpu.VMEM((size, size), jnp.float32)] * count,
        in_specs=[smem, vmem, vmem, vmem],
        out_specs=[vmem] * count,
        scratch_shapes=[pltpu.VMEM((size, size), jnp.float32)] * count,
        cost_estimate=pl.CostEstimate(flops=15 * 10**9, bytes_accessed=8 * count * size**2, transcendentals=0),
        compiler_params=pltpu.CompilerParams(vmem_limit_bytes=GRANT),
        name="factor_inverse",
    )(core, gram, mine, other)


def near_kernel(groups, first_slot, spots, sketched, index_ref, count_ref, flag_ref, blocks_ref, base_ref, *refs):
    pieces = refs[:groups]
    sketch_ref = refs[groups] if sketched else None
    rest = refs[groups + sketched :]
    out_ref, ext = rest[0], rest[-1]
    block_count, slot_count, size, _ = blocks_ref.shape
    at = 0
    for g in range(groups):
        depth = pieces[g].shape[0]
        ext[at : at + depth, :] = pieces[g][...]
        at += depth
    out_ref[...] = base_ref[...]
    for b in range(block_count):
        rows = pl.ds(b * size, size)
        for j in range(first_slot, slot_count):
            spot = index_ref[b, j]
            start = jnp.int32(0)
            here = jnp.bool_(False)
            for order, name in enumerate(spots):
                same = spot == name
                start = jnp.where(same, order * size, start)
                here = here | same

            @pl.when(here & (j < count_ref[b]))
            def _(b=b, j=j, rows=rows, start=start):
                piece = ext[pl.ds(pl.multiple_of(start, size), size), :]
                out_ref[rows, :] -= dot3(blocks_ref[b, j], piece, NN)

    if sketched:
        rest[1][...] = dot3(out_ref[...], sketch_ref[...], NN)


def near_step(blocks, base, pieces, spots, index, count, flag, first_slot, sketch=None):
    block_count, slot_count, size, _ = blocks.shape
    rows, width = base.shape
    total = sum(piece.shape[0] for piece in pieces)
    vmem = pl.BlockSpec(memory_space=pltpu.VMEM)
    smem = pl.BlockSpec(memory_space=pltpu.SMEM)
    extra = [] if sketch is None else [sketch]
    shapes = [(rows, width)] + [(rows, value.shape[1]) for value in extra]
    return pl.pallas_call(
        functools.partial(near_kernel, len(pieces), first_slot, tuple(spots), len(extra)),
        out_shape=[pltpu.VMEM(shape, jnp.float32) for shape in shapes],
        in_specs=[smem] * 3 + [vmem] * (2 + len(pieces) + len(extra)),
        out_specs=[vmem] * len(shapes),
        scratch_shapes=[pltpu.VMEM((total, width), jnp.float32)],
        cost_estimate=pl.CostEstimate(
            flops=6 * block_count * slot_count * size * size * width,
            bytes_accessed=4 * (total * width + 2 * rows * width + blocks.size),
            transcendentals=0,
        ),
        compiler_params=pltpu.CompilerParams(vmem_limit_bytes=GRANT),
        name="near_step",
    )(index, count, flag, blocks, base, *pieces, *extra)


def leaf_kernel(flag_ref, half_ref, other_ref, far_ref, sketch_ref, gram_ref, part_ref, keep_ref, send_ref, product):
    sketch = half_ref[...] + other_ref[...] if other_ref is not None else half_ref[...]
    sketch_ref[...] = sketch
    turned = sketch.T
    gram = dot3(turned, sketch, NN)
    gram_ref[...] = gram
    rank = gram.shape[0]
    width = part_ref.shape[1]
    part_ref[...] = jnp.where(flag_ref[0] == 1, gram[:, rank - width :], gram[:, :width])
    product[...] = dot3(turned, far_ref[...], NN)
    depth = keep_ref.shape[0]
    keep_ref[...] = product[pl.ds(pl.multiple_of(flag_ref[1], depth), depth), :]
    send_ref[...] = product[pl.ds(pl.multiple_of(flag_ref[2], depth), depth), :]


def leaf_products(flag, part, other, far):
    rows, rank = part.shape
    width = far.shape[1]
    vmem = pl.BlockSpec(memory_space=pltpu.VMEM)
    smem = pl.BlockSpec(memory_space=pltpu.SMEM)
    half = rank // 2
    shapes = [(rows, rank), (rank, rank), (rank, rank if other is None else half), (half, width), (half, width)]
    kernel = leaf_kernel
    args = [flag, part, other, far]
    if other is None:
        args = [flag, part, far]

        def kernel(flag_ref, part_ref, far_ref, *refs):
            leaf_kernel(flag_ref, part_ref, None, far_ref, *refs)

    return pl.pallas_call(
        kernel,
        out_shape=[pltpu.VMEM(shape, jnp.float32) for shape in shapes],
        in_specs=[smem] + [vmem] * (len(args) - 1),
        out_specs=[vmem] * len(shapes),
        scratch_shapes=[pltpu.VMEM((rank, width), jnp.float32)],
        cost_estimate=pl.CostEstimate(
            flops=6 * rows * rank * (rank + width), bytes_accessed=4 * rows * (3 * rank + width), transcendentals=0
        ),
        compiler_params=pltpu.CompilerParams(vmem_limit_bytes=GRANT),
        name="leaf_products",
    )(*args)


def staged(stage, flag_ref, mine, other):
    depth = mine.shape[0]
    stage[pl.ds(pl.multiple_of(flag_ref[1], depth), depth), :] = mine
    stage[pl.ds(pl.multiple_of(flag_ref[2], depth), depth), :] = other
    return stage[...]


def early_kernel(flag_ref, *refs):
    count = LEVELS - 1
    inverses, mine_ref, other_ref = refs[:count], refs[count], refs[count + 1]
    out_ref, stage, result, sems = refs[count + 2 :]
    copies = []
    for h in range(count):
        result[h] = dot3(inverses[h][...], staged(stage.at[h], flag_ref, mine_ref[h], other_ref[h]), NN)
        copies.append(pltpu.make_async_copy(result.at[h], out_ref.at[h, 0], sems.at[h]))
        copies[-1].start()
    for copy in copies:
        copy.wait()


def reduce_early(flag, inverses, mine, other):
    rank, width = inverses[0].shape[0], mine.shape[2]
    vmem = pl.BlockSpec(memory_space=pltpu.VMEM)
    smem = pl.BlockSpec(memory_space=pltpu.SMEM)
    count = LEVELS - 1
    return pl.pallas_call(
        early_kernel,
        out_shape=jax.ShapeDtypeStruct((LEVELS, 1, rank, width), jnp.float32),
        in_specs=[smem] + [vmem] * (count + 2),
        out_specs=pl.BlockSpec(memory_space=pl.ANY),
        scratch_shapes=[
            pltpu.VMEM((count, rank, width), jnp.float32),
            pltpu.VMEM((count, rank, width), jnp.float32),
            pltpu.SemaphoreType.DMA((count,)),
        ],
        cost_estimate=pl.CostEstimate(
            flops=6 * count * rank * rank * width, bytes_accessed=8 * count * rank * (rank + width), transcendentals=0
        ),
        compiler_params=pltpu.CompilerParams(vmem_limit_bytes=GRANT),
        name="reduce_early",
    )(flag, *inverses, mine, other)


def last_kernel(flag_ref, inverse_ref, mine_ref, other_ref, kept_ref, out_ref, stage, result, sem):
    value = staged(stage, flag_ref, mine_ref[...], other_ref[...])
    half = result.shape[0] // 2
    copies = []
    for part in range(2):
        rows = pl.ds(part * half, half)
        result[rows, :] = dot3(inverse_ref[rows, :], value, NN)
        copies.append(pltpu.make_async_copy(result.at[rows], out_ref.at[LEVELS - 1, 0, rows], sem.at[part]))
        copies[-1].start()
    for copy in copies:
        copy.wait()


def reduce_last(flag, inverse, mine, other, reduced):
    rank, width = inverse.shape[0], mine.shape[1]
    vmem = pl.BlockSpec(memory_space=pltpu.VMEM)
    smem = pl.BlockSpec(memory_space=pltpu.SMEM)
    hbm = pl.BlockSpec(memory_space=pl.ANY)
    return pl.pallas_call(
        last_kernel,
        out_shape=jax.ShapeDtypeStruct(reduced.shape, jnp.float32),
        in_specs=[smem] + [vmem] * 3 + [hbm],
        out_specs=hbm,
        scratch_shapes=[
            pltpu.VMEM((rank, width), jnp.float32),
            pltpu.VMEM((rank, width), jnp.float32),
            pltpu.SemaphoreType.DMA((2,)),
        ],
        input_output_aliases={4: 0},
        cost_estimate=pl.CostEstimate(
            flops=6 * rank * rank * width, bytes_accessed=8 * rank * (rank + width), transcendentals=0
        ),
        compiler_params=pltpu.CompilerParams(vmem_limit_bytes=GRANT),
        name="reduce_last",
    )(flag, inverse, mine, other, reduced)


def across(value, axis, bit):
    return lax.ppermute(value, axis, [(i, i ^ 1 << bit) for i in range(lax.axis_size(axis))])


def relayed(value, axis):
    count = lax.axis_size(axis)
    steps = [(i, i + 2 if i % 2 == 0 else i - 2) for i in range(count)]
    return lax.ppermute(value, axis, [(i, t) for i, t in steps if 0 <= t < count])


def leaf_and_levels(samples, probes, near_blocks, near_cols, near_count, sketch):
    rows_dev, _ = samples.shape
    block_size = near_blocks.shape[2]
    block_count = rows_dev // block_size
    rank = sketch.shape[1]
    position = lax.axis_index("rows")
    bits = [position >> h & 1 for h in range(LEVELS)]
    odd = bits[0] == 1
    halves = 2 if lax.axis_size("samp") == 2 else 1
    core = lax.axis_index("samp") % 2
    half = rank // 2
    flag = jnp.stack([core, bits[0] * half, half - bits[0] * half]).astype(jnp.int32)

    index = near_cols - (position * block_count - block_count)
    moved = jnp.where(index < block_count, 2 * block_count, jnp.where(index >= 2 * block_count, -2 * block_count, 0))
    index = index + jnp.where(odd, moved, 0)

    parts = block_count * SPLIT
    depth = rows_dev // parts
    later = lax.optimization_barrier(probes)
    pieces = [(later if i else probes)[i * depth : (i + 1) * depth] for i in range(parts)]
    peer = [across(pieces[i], "rows", 0) for i in range(parts)]
    far = [relayed(peer[i], "rows") for i in range(parts)]

    early = (block_count - 1) * SPLIT
    spots = [*range(block_count - 1), *range(block_count, 3 * block_count)]
    oldest = pltpu.with_memory_space_constraint(peer[0], pltpu.HBM)
    landed = far[:early] + [probes, oldest] + peer[1:]
    (left,) = near_step(near_blocks, samples, landed, spots, index, near_count, flag, 0)
    spots = [block_count - 1]
    far_samples, partial = near_step(near_blocks, left, far[early:], spots, index, near_count, flag, 1, sketch)
    if halves == 2:
        other = across(partial, "samp", 0)
    else:
        partial, other = lax.psum(partial, "samp"), None
    leaf_sketch, gram, part, keep, send = leaf_products(flag, partial, other, far_samples)

    sums = []
    for h in range(LEVELS):
        part = part + across(part, "rows", h)
        sums.append(part)
    sums = jnp.stack(sums)
    sums_other = across(sums, "samp", 0) if halves == 2 else sums
    leaf_inverse, *inverses = factor_inverse(flag, gram, sums, sums_other)
    leaf_basis = lax.dot_general(leaf_sketch, leaf_inverse, (NT, ((), ())), precision=HIGH)

    value = keep + across(send, "rows", 0)
    values = [value]
    for h in range(1, LEVELS):
        value = value + across(value, "rows", h)
        values.append(value)
    lower = jnp.stack(values[:-1])
    lower_other = across(lower, "rows", 0)
    last_other = across(value, "rows", 0)
    reduced = reduce_early(flag, inverses[:-1], lower, lower_other)
    reduced = reduce_last(flag, inverses[-1], value, last_other, reduced)
    return (leaf_basis, reduced)


def solution(mesh):
    return jax.shard_map(
        leaf_and_levels,
        mesh=mesh,
        in_specs=(
            P("rows", "samp"),
            P("rows", "samp"),
            P("rows", None, None, None),
            P("rows", None),
            P("rows"),
            P("samp", None),
        ),
        out_specs=(P("rows", None), P(None, "rows", None, "samp")),
        check_vma=False,
    )
```
